32 devices in a mesh: elem: 8 (over z, core), front: 4 (over y, x).
Axes of the slice: x: 2, y: 2, z: 4, core: 2. Of those that a mesh axis runs over, the one named last changes fastest.
Arguments:
- elem_mat: bfloat16 [24, 24, 4096], P(None, None, ('elem', 'front')), may hold values from -1.25 to 1.25
- elem_deriv: bfloat16 [24, 24, 4096], P(None, None, ('elem', 'front')), may hold values from -1.1953125 to 1.1953125
- elem_disp: bfloat16 [24, 4096], P(None, ('elem', 'front')), may hold values from -6 to 6
- elem_sens: bfloat16 [4096, 24, 512], P(('elem', 'front')), may hold values from -3 to 3
- design_var: int32 [4096], P(('elem', 'front')), may hold values from 0 to 511
- dof_rows: int32 [24, 4096], P(None, ('elem', 'front')), may hold values from 0 to 14336, as said below
- inverse_factor: bfloat16 [57344, 8192], P('front', 'elem'), may hold values from -2 to 2
- coupling: bfloat16 [8192, 49152], P('elem', 'front'), may hold values from -0.0625 to 0.0625
- front_sizes: int32 [7], replicated, may hold values from 4096 to 8192
Outputs:
- sens: float32 [57344, 512], P('front', 'elem')
The draws below stay inside these ranges and needn't reach their ends.
Inputs may be any that keep to these rules, and one draw needn't show every extreme that they name: `dof_rows`: the used rows of one element lie in one aligned block of 128 rows; the value 14336 marks a degree of freedom that no front holds.
All inputs are finite; a program needn't handle non-finite values.
Results may differ from the reference program's by a relative error of at most 0.014.
Values may be sent and summed in bfloat16 or wider, within the bound.
A program may use at most 128 MiB of HBM per device.

```python
import jax
import jax.numpy as jnp
from jax import lax

DOF = 24
NRHS = 512
FS = 8192
LEVELS = 3
BLK = 128
E_DEV = 128
ELEMS = 4096
LR = 14336
CR = 12288
FRONTS = 7
N_FRONT = 4


def draw_dof_rows(key, part):
    key_block = jax.random.fold_in(key, 11)
    key_offset = jax.random.fold_in(key, 12)
    key_unused = jax.random.fold_in(key, 13)
    block_index = jax.random.randint(key_block, (1, ELEMS), 0, LR // BLK)
    offsets = jax.random.randint(key_offset, (DOF, ELEMS), 0, BLK)
    unused = jax.random.randint(key_unused, (DOF, ELEMS), 0, 8)
    places = block_index * BLK + offsets
    return jnp.where(unused == 0, LR, places).astype(jnp.int32)


def draw_inverse_factor(key, part):
    total_rows = N_FRONT * LR
    row_at = jnp.arange(total_rows, dtype=jnp.int32)
    device_at = row_at // LR
    spot_at = row_at % LR
    global_row = jnp.zeros_like(row_at)
    start_spot = 0
    for level_at in range(LEVELS):
        share_count = N_FRONT >> LEVELS - 1 - level_at
        block_rows = FS // share_count
        inside = (spot_at >= start_spot) & (spot_at < start_spot + block_rows)
        global_row = jnp.where(inside, device_at % share_count * block_rows + spot_at - start_spot, global_row)
        start_spot = start_spot + block_rows
    key_off = jax.random.fold_in(key, 21)
    key_diag = jax.random.fold_in(key, 22)
    spread_part = jax.random.normal(key_off, (total_rows, FS), jnp.float32) * (0.5 / FS ** 0.5)
    diag_part = jax.random.uniform(key_diag, (total_rows,), jnp.float32, 0.6, 1.2)
    spread_part = jnp.clip(spread_part, -1.0, 1.0)
    columns_at = jnp.arange(FS, dtype=jnp.int32)
    on_diag = (columns_at[None, :] == global_row[:, None]).astype(jnp.float32)
    return (spread_part * (1.0 - on_diag) + on_diag * diag_part[:, None]).astype(jnp.bfloat16)


def place_ends(result, key, least, largest):
    spot = [jax.random.randint(jax.random.fold_in(key, axis), (), 0, length) for axis, length in enumerate(result.shape)]
    widest = result.shape.index(max(result.shape))
    next_to = spot[:widest] + [(spot[widest] + 1) % result.shape[widest]] + spot[widest + 1:]
    return result.at[tuple(spot)].set(least).at[tuple(next_to)].set(largest)


def block_scale(stream_key, dims, cuts, least, high):
    factor_of, own = 1.0, jax.random.fold_in(stream_key, 6)
    for position, blocks in cuts:
        draws = jnp.exp(jax.random.uniform(jax.random.fold_in(own, position), (blocks,), jnp.float32, least / len(cuts), high / len(cuts)))
        factor_of = factor_of * jnp.repeat(draws, dims[position] // blocks).reshape([-1 if axis == position else 1 for axis in range(len(dims))])
    return factor_of


def gaussian(rng, extent, scale, reach, shards=(), kind=jnp.bfloat16):
    entries = jax.random.normal(rng, extent, jnp.float32) * scale
    if len(shards) > 0:
        entries = block_scale(rng, extent, shards, -0.22, 0.18) * entries
    return jnp.clip(entries, min=-reach, max=reach).astype(kind)


def setup_inputs(seed: int = 0) -> dict:
    key_of = jax.random.split(jax.random.key(seed), 10)
    return {
        "elem_mat": gaussian(key_of[0], (DOF, DOF, ELEMS), DOF ** -0.5, 1.25, ((2, 32),)),
        "elem_deriv": gaussian(key_of[1], (DOF, DOF, ELEMS), 0.2, 1.1953125, ((2, 32),)),
        "elem_disp": gaussian(key_of[2], (DOF, ELEMS), 1.0, 6.0, ((1, 32),)),
        "elem_sens": gaussian(key_of[3], (ELEMS, DOF, NRHS), 0.5, 3.0, ((0, 32),)),
        "design_var": place_ends(jax.random.randint(key_of[4], (ELEMS,), 0, NRHS), jax.random.fold_in(key_of[4], 1), 0, NRHS - 1).astype(jnp.int32),
        "dof_rows": draw_dof_rows(jax.random.fold_in(key_of[9], 71), 0),
        "inverse_factor": draw_inverse_factor(jax.random.fold_in(key_of[9], 71), 0),
        "coupling": gaussian(key_of[7], (FS, N_FRONT * CR), FS ** -0.5, 0.0625, ((0, 8), (1, 4))),
        "front_sizes": place_ends(jax.random.randint(key_of[8], (FRONTS,), FS // 2, FS + 1), jax.random.fold_in(key_of[8], 1), FS // 2, FS).astype(jnp.int32),
    }


def level_shape(level_at):
    share_count = N_FRONT >> (LEVELS - 1 - level_at)
    return share_count, FS // share_count


def level_offset(level_at):
    return sum(level_shape(other)[1] for other in range(level_at))


def take_level(matrix, level_at):
    share_count, block_rows = level_shape(level_at)
    offset = level_offset(level_at)
    sliced = matrix.reshape(N_FRONT, LR, matrix.shape[-1])[:, offset:offset + block_rows]
    return sliced.reshape(N_FRONT // share_count, FS, matrix.shape[-1])


def couple_level(coupling, level_at):
    share_count, block_rows = level_shape(level_at)
    offset = level_offset(level_at)
    sliced = coupling.reshape(FS, N_FRONT, CR)[:, :, offset:offset + block_rows]
    return sliced.reshape(FS, N_FRONT // share_count, FS).transpose(1, 0, 2)


def level_mask(front_sizes, level_at):
    front_count = 2 ** (LEVELS - 1 - level_at)
    first_front = sum(2 ** (LEVELS - 1 - other) for other in range(level_at))
    live_sizes = front_sizes[first_front:first_front + front_count]
    rows_at = jnp.arange(FS, dtype=jnp.int32)
    return (rows_at[None, :, None] < live_sizes[:, None, None]).astype(jnp.float32)


def reference(elem_mat, elem_deriv, elem_disp, elem_sens, design_var, dof_rows, inverse_factor, coupling, front_sizes):
    def add_block(totals, block_index):
        start_row = block_index * E_DEV
        tables = lax.dynamic_slice_in_dim(elem_mat, start_row, E_DEV, 2).astype(jnp.float32)
        derivs = lax.dynamic_slice_in_dim(elem_deriv, start_row, E_DEV, 2).astype(jnp.float32)
        disps = lax.dynamic_slice_in_dim(elem_disp, start_row, E_DEV, 1).astype(jnp.float32)
        sens_block = lax.dynamic_slice_in_dim(elem_sens, start_row, E_DEV, 0).astype(jnp.float32)
        variables = lax.dynamic_slice_in_dim(design_var, start_row, E_DEV, 0)
        places = lax.dynamic_slice_in_dim(dof_rows, start_row, E_DEV, 1).T
        pseudo = -jnp.einsum("ije,ejc->eic", tables, sens_block)
        drive_term = -jnp.einsum("ije,je->ei", derivs, disps)
        hit_column = (jnp.arange(NRHS, dtype=jnp.int32)[None, :] == variables[:, None]).astype(jnp.float32)
        pseudo = pseudo + drive_term[:, :, None] * hit_column[:, None, :]
        front_index = block_index % N_FRONT
        places = jnp.where(places < LR, places + front_index * LR, N_FRONT * LR).astype(jnp.int32)
        totals = totals.at[places.reshape(-1)].add(pseudo.reshape(-1, NRHS), mode="drop")
        return totals, None

    start_loads = jnp.zeros((N_FRONT * LR, NRHS), jnp.float32)
    loads, _ = lax.scan(add_block, start_loads, jnp.arange(ELEMS // E_DEV, dtype=jnp.int32))

    forward_out = []
    acc_rows = None
    for level_at in range(LEVELS):
        live_rows = level_mask(front_sizes, level_at)
        factor_rows = take_level(inverse_factor, level_at).astype(jnp.float32)
        given = take_level(loads, level_at)
        if acc_rows is not None:
            given = given - acc_rows
        rhs_in = (live_rows * given).astype(jnp.bfloat16)
        solved = live_rows * jnp.einsum("nij,njc->nic", factor_rows, rhs_in.astype(jnp.float32))
        forward_out.append(solved)
        if level_at < LEVELS - 1:
            links = couple_level(coupling, level_at).astype(jnp.float32)
            rounded = solved.astype(jnp.bfloat16).astype(jnp.float32)
            partial_value = jnp.einsum("nij,njc->nic", links, rounded)
            acc_rows = partial_value.reshape(partial_value.shape[0] // 2, 2, FS, NRHS).sum(axis=1)

    pieces_out = [None] * LEVELS
    parent_rows = None
    for level_at in reversed(range(LEVELS)):
        live_rows = level_mask(front_sizes, level_at)
        factor_rows = take_level(inverse_factor, level_at).astype(jnp.float32)
        residual = forward_out[level_at]
        if parent_rows is not None:
            links = couple_level(coupling, level_at).astype(jnp.float32)
            spread_parent = jnp.repeat(parent_rows.astype(jnp.float32), 2, axis=0)
            residual = residual - jnp.einsum("nji,njc->nic", links, spread_parent)
        back_in = (live_rows * residual).astype(jnp.bfloat16)
        answer = live_rows * jnp.einsum("nji,njc->nic", factor_rows, back_in.astype(jnp.float32))
        pieces_out[level_at] = answer
        parent_rows = answer.astype(jnp.bfloat16)

    laid_out = [pieces_out[level_at].reshape(N_FRONT, level_shape(level_at)[1], NRHS) for level_at in range(LEVELS)]
    return jnp.concatenate(laid_out, axis=1).reshape(N_FRONT * LR, NRHS)
```

```python
import jax
import jax.numpy as jnp
from jax import lax
from jax.experimental import pallas as pl
from jax.experimental.pallas import tpu as pltpu
from jax.sharding import PartitionSpec as P

LEVELS = 3
CHUNKS = 4
PAIR = 2
BLK = 128
GROUP = 8
BF, F32 = jnp.bfloat16, jnp.float32


def local_pseudo(tables, derivs, disps, sens, variables, column_ids):
    pseudo = -jnp.einsum("ije,ejc->eic", tables, sens, preferred_element_type=F32)
    drive_term = -jnp.einsum("ije,je->ei", derivs, disps, preferred_element_type=F32)
    hit_column = (column_ids[None, :] == variables[:, None]).astype(F32)
    return pseudo + drive_term[:, :, None] * hit_column[:, None, :]


def scatter_kernel(blocks_ref, rows_ref, own_ref, other_ref, out_ref):
    out_ref[...] = jnp.zeros_like(out_ref)
    count, dof = own_ref.shape[0], rows_ref.shape[1]

    for source_at, source_ref in enumerate((own_ref, other_ref)):

        def step(group_at, carry):
            first = pl.multiple_of(group_at * GROUP, GROUP)
            entry = pl.multiple_of(source_at * count + first, GROUP)
            rows = rows_ref[pl.ds(entry, GROUP), :]
            spread = []
            for at in range(GROUP):
                lanes = jnp.broadcast_to(rows[at : at + 1, :], (BLK, dof))
                hits = lax.broadcasted_iota(jnp.int32, (BLK, dof), 0) == lanes
                spread.append(
                    jnp.dot(hits.astype(F32).astype(BF), source_ref[first + at], preferred_element_type=F32)
                )
            for at in range(GROUP):
                block = blocks_ref[entry + at]
                out_ref[block] = out_ref[block] + spread[at]
            return carry

        lax.fori_loop(0, count // GROUP, step, 0)


def block_places(places, spot_rows):
    places = places.T
    used = places < spot_rows
    blocks = jnp.min(jnp.where(used, places, spot_rows), 1) // BLK
    blocks = jnp.clip(blocks, 0, spot_rows // BLK - 1)
    rows = jnp.where(used, places - blocks[:, None] * BLK, -1)
    return blocks, rows


def scatter_rows(own, other, pair_at, blocks, rows, spot_rows):
    count, dof, width = own.shape
    lanes = width * PAIR // CHUNKS
    block_count = spot_rows // BLK
    piece = pl.BlockSpec((count, dof, lanes), lambda i: (0, 0, pair_at))
    spread = pl.pallas_call(
        scatter_kernel,
        grid=(1,),
        out_shape=jax.ShapeDtypeStruct((block_count, BLK, lanes), F32),
        in_specs=[
            pl.BlockSpec(memory_space=pltpu.SMEM),
            pl.BlockSpec(rows.shape, lambda i: (0, 0)),
            piece,
            piece,
        ],
        out_specs=pl.BlockSpec((block_count, BLK, lanes), lambda i: (0, 0, 0)),
        compiler_params=pltpu.CompilerParams(vmem_limit_bytes=40 * 1024 * 1024),
    )(blocks, rows, own, other)
    return spread.reshape(spot_rows, lanes)


def body(
    elem_mat, elem_deriv, elem_disp, elem_sens, design_var, dof_rows, inverse_factor, coupling, front_sizes
):
    depth_bits = lax.axis_size("front").bit_length() - 1
    elem_count = lax.axis_size("elem")
    z_count = elem_count // 2
    device = lax.axis_index("front")
    elem_at = lax.axis_index("elem")
    z_at, core_at = elem_at // 2, elem_at % 2
    inner = coupling.shape[0]
    solve_size = inner * elem_count
    spot_rows = inverse_factor.shape[0]
    columns = elem_sens.shape[2]
    own_columns = columns // elem_count
    grain = own_columns // CHUNKS
    half = z_count * grain

    def core_swap(value):
        return lax.ppermute(value, "elem", [(i, i ^ 1) for i in range(elem_count)])

    def hop(value, pairs):
        steps = [(2 * a + c, 2 * b + c) for a, b in pairs for c in range(2)]
        return lax.ppermute(value, "elem", steps)

    def front_swap(value, bit):
        return lax.ppermute(value, "front", [(i, i ^ 1 << bit) for i in range(lax.axis_size("front"))])

    def in_group(value, share):
        count = lax.axis_size("front")
        groups = [list(range(i, i + share)) for i in range(0, count, share)]
        return lax.all_to_all(value, "front", split_axis=0, concat_axis=0, tiled=True, axis_index_groups=groups)

    facts = []
    offset = 0
    first_front = 0
    for level_at in range(LEVELS):
        bit_count = depth_bits - (LEVELS - 1 - level_at)
        block_rows = solve_size >> bit_count
        front_id = first_front + (device >> bit_count)
        size_now = lax.dynamic_index_in_dim(front_sizes, front_id, 0, keepdims=False)
        start = (device & (1 << bit_count) - 1) * block_rows
        row_live = (start + lax.iota(jnp.int32, block_rows) < size_now).astype(F32)[None, :]
        inner_live = (elem_at * inner + lax.iota(jnp.int32, inner) < size_now).astype(F32)[None, :]
        facts.append((bit_count, block_rows, offset, row_live, inner_live))
        offset = offset + block_rows
        first_front = first_front + (1 << LEVELS - 1 - level_at)

    place = lax.iota(jnp.int32, columns)
    place_core, rest = place // (z_count * own_columns), place % (z_count * own_columns)
    place_chunk, rest = rest // half, rest % half
    column_ids = (rest // grain * 2 + place_core) * own_columns + place_chunk * grain + rest % grain
    order = (place[:, None] == column_ids[None, :]).astype(BF)
    sens = jnp.einsum("ejc,cd->ejd", elem_sens, order, preferred_element_type=F32).astype(BF)

    pseudo = local_pseudo(elem_mat, elem_deriv, elem_disp, sens, design_var, column_ids).astype(BF)
    side = columns // 2
    own_pseudo = lax.dynamic_slice_in_dim(pseudo, core_at * side, side, 2)
    other_pseudo = core_swap(lax.dynamic_slice_in_dim(pseudo, (1 - core_at) * side, side, 2))
    places = jnp.concatenate([dof_rows, core_swap(dof_rows)], 1)
    blocks, rows = block_places(places, spot_rows)

    def chain_scatter(value):
        for s in range(z_count - 1):
            up, down = value[s + 1 :], value[: z_count - 1 - s]
            sent = jnp.where(z_at == s, up, down).astype(BF)
            got = hop(sent, [(s, s + 1), (z_count - 1 - s, z_count - 2 - s)]).astype(F32)
            is_up, is_down = z_at == s + 1, z_at == z_count - 2 - s
            gap = jnp.zeros((s + 1,) + value.shape[1:], F32)
            raised = jnp.where(is_up, jnp.concatenate([gap, got]), jnp.concatenate([got, gap]))
            value = value + jnp.where(is_up | is_down, raised, 0.0)
        return lax.dynamic_index_in_dim(value, z_at, 0, keepdims=False)

    given = [[None] * CHUNKS for _ in range(LEVELS)]

    def load_level(spread, pair_at, level_at):
        bit_count, block_rows, offset, row_live, inner_live = facts[level_at]
        piece = spread[offset : offset + block_rows]
        lanes = piece.shape[1]
        share = 1 << bit_count
        depth = inner // share
        if share > 1:
            piece = piece.reshape(elem_count // share, share, depth, lanes).swapaxes(0, 1)
            piece = in_group(piece.astype(BF), share).astype(F32)
        mine = chain_scatter(piece.reshape(z_count, 2 * depth, lanes)).astype(BF)
        own = lax.dynamic_slice_in_dim(mine, core_at * depth, depth, 0)
        other = core_swap(lax.dynamic_slice_in_dim(mine, (1 - core_at) * depth, depth, 0))
        both = jnp.concatenate([own.T.reshape(PAIR, half, depth), other.T.reshape(PAIR, half, depth)], 1)
        if share > 1:
            at = (device & share - 1) * depth
            both = lax.dynamic_update_slice_in_dim(jnp.zeros((PAIR, 2 * half, inner), BF), both, at, 2)
        for i in range(PAIR):
            given[level_at][pair_at * PAIR + i] = both[i]

    spreads = []
    for pair_at in range(CHUNKS // PAIR):
        spreads.append(scatter_rows(own_pseudo, other_pseudo, pair_at, blocks, rows, spot_rows))
        for level_at in range(LEVELS):
            load_level(spreads[pair_at], pair_at, level_at)

    def sum_group(value, bit_count):
        for bit_at in range(bit_count):
            value = value + front_swap(value.astype(BF), bit_at).astype(F32)
        return value

    middle = z_count // 2

    def chain_sum(product, finish):
        total = product[:half] + core_swap(product[half:].astype(BF)).astype(F32)
        for i in range(middle - 1):
            total = total + hop(total.astype(BF), [(i, i + 1), (z_count - 1 - i, z_count - 2 - i)]).astype(F32)
        sent = total.astype(BF)
        got = hop(sent, [(middle - 1, middle), (middle, middle - 1)])
        whole = finish(sent.astype(F32) + got.astype(F32))
        wide = whole.astype(BF)
        for i in reversed(range(middle - 1)):
            got = hop(wide, [(i + 1, i), (z_count - 2 - i, z_count - 1 - i)])
            wide = jnp.where((z_at == i) | (z_at == z_count - 1 - i), got, wide)
        return whole, jnp.concatenate([wide, core_swap(wide)], 0)

    def contract(left, right, axis):
        return lax.dot_general(left, right, (((1,), (axis,)), ((), ())), preferred_element_type=F32)

    def forward(chunk, level_at, state):
        bit_count, block_rows, offset, row_live, inner_live = facts[level_at]
        part = given[level_at][chunk].astype(F32)
        if level_at:
            below = facts[level_at - 1]
            part = part - contract(state["wide"], coupling[:, below[2] : below[2] + below[1]], 1)
        rhs = (inner_live * sum_group(part, bit_count)).astype(BF)
        product = contract(rhs, inverse_factor[offset : offset + block_rows], 1)
        state[level_at], state["wide"] = chain_sum(product, lambda whole: row_live * whole)

    def answer(level_at, state):
        bit_count, block_rows, offset, row_live, inner_live = facts[level_at]
        partial = contract(state["wide"], inverse_factor[offset : offset + block_rows], 0)
        state["x"] = (inner_live * sum_group(partial, bit_count)).astype(BF)
        state["x", level_at] = state["x"]

    def backward(chunk, level_at, state):
        bit_count, block_rows, offset, row_live, inner_live = facts[level_at]
        product = contract(state["x"], coupling[:, offset : offset + block_rows], 0)
        held = state[level_at]
        _, state["wide"] = chain_sum(product, lambda whole: row_live * (held - whole))

    states = [{} for _ in range(CHUNKS)]
    for level_at in range(LEVELS):
        for chunk in range(CHUNKS):
            forward(chunk, level_at, states[chunk])
    for level_at in reversed(range(LEVELS)):
        for chunk in range(CHUNKS):
            if level_at < LEVELS - 1:
                backward(chunk, level_at, states[chunk])
            answer(level_at, states[chunk])

    def piece_of(level_at):
        bit_count, block_rows = facts[level_at][:2]
        share = 1 << bit_count
        depth = inner // share
        whole = jnp.stack([state["x", level_at] for state in states])
        if share > 1:
            at = (device & share - 1) * depth
            whole = lax.dynamic_slice_in_dim(whole, at, depth, 2)
        own, other = whole[:, :half], core_swap(whole[:, half:])
        first = jnp.where(core_at == 0, own, other)
        second = jnp.where(core_at == 0, other, own)
        both = jnp.stack([first, second], 2).reshape(CHUNKS, z_count, grain, 2, depth)
        both = both.transpose(1, 0, 2, 3, 4)
        groups = [[2 * z + c for z in range(z_count)] for c in range(2)]
        turned = lax.all_to_all(both, "elem", split_axis=0, concat_axis=0, tiled=True, axis_index_groups=groups)
        turned = turned.reshape(z_count, own_columns, 2, depth).swapaxes(1, 2).reshape(elem_count, own_columns, depth)
        if share > 1:
            turned = in_group(turned.reshape(share, elem_count // share, own_columns, depth), share)
            turned = turned.swapaxes(0, 1)
            turned = turned.transpose(0, 1, 3, 2).reshape(block_rows, own_columns)
        else:
            turned = turned.transpose(0, 2, 1).reshape(block_rows, own_columns)
        return turned

    return jnp.concatenate([piece_of(level_at) for level_at in range(LEVELS)], 0).astype(F32)


def solution(mesh):
    return jax.shard_map(
        body,
        mesh=mesh,
        in_specs=(
            P(None, None, ("elem", "front")),
            P(None, None, ("elem", "front")),
            P(None, ("elem", "front")),
            P(("elem", "front"), None, None),
            P(("elem", "front")),
            P(None, ("elem", "front")),
            P("front", "elem"),
            P("elem", "front"),
            P(),
        ),
        out_specs=P("front", "elem"),
        check_vma=False,
    )
```

```python
import functools

import jax
import jax.numpy as jnp
from jax import lax
from jax.experimental import pallas as pl
from jax.experimental.pallas import tpu as pltpu
from jax.sharding import PartitionSpec as P

LEVELS = 3
CHUNKS = 2
PAIR = 1
TILE = 512
RING = 3
HELD = 8
BLK = 128
GROUP = 8
BF, F32 = jnp.bfloat16, jnp.float32


def local_pseudo(tables, derivs, disps, sens, variables, column_ids):
    pseudo = -jnp.einsum("ije,ejc->eic", tables, sens, preferred_element_type=F32)
    drive_term = -jnp.einsum("ije,je->ei", derivs, disps, preferred_element_type=F32)
    hit_column = (column_ids[None, :] == variables[:, None]).astype(F32)
    return pseudo + drive_term[:, :, None] * hit_column[:, None, :]


def scatter_kernel(blocks_ref, rows_ref, own_ref, other_ref, out_ref):
    out_ref[...] = jnp.zeros_like(out_ref)
    count, dof = own_ref.shape[0], rows_ref.shape[1]

    for source_at, source_ref in enumerate((own_ref, other_ref)):

        def step(group_at, carry):
            first = pl.multiple_of(group_at * GROUP, GROUP)
            entry = pl.multiple_of(source_at * count + first, GROUP)
            rows = rows_ref[pl.ds(entry, GROUP), :]
            spread = []
            for at in range(GROUP):
                lanes = jnp.broadcast_to(rows[at : at + 1, :], (BLK, dof))
                hits = lax.broadcasted_iota(jnp.int32, (BLK, dof), 0) == lanes
                spread.append(
                    jnp.dot(hits.astype(F32).astype(BF), source_ref[first + at], preferred_element_type=F32)
                )
            for at in range(GROUP):
                block = blocks_ref[entry + at]
                out_ref[block] = out_ref[block] + spread[at]
            return carry

        lax.fori_loop(0, count // GROUP, step, 0)


def block_places(places, spot_rows):
    places = places.T
    used = places < spot_rows
    blocks = jnp.min(jnp.where(used, places, spot_rows), 1) // BLK
    blocks = jnp.clip(blocks, 0, spot_rows // BLK - 1)
    rows = jnp.where(used, places - blocks[:, None] * BLK, -1)
    return blocks, rows


def scatter_rows(own, other, pair_at, blocks, rows, spot_rows):
    count, dof, width = own.shape
    lanes = width * PAIR // CHUNKS
    block_count = spot_rows // BLK
    piece = pl.BlockSpec((count, dof, lanes), lambda i: (0, 0, pair_at))
    spread = pl.pallas_call(
        scatter_kernel,
        grid=(1,),
        out_shape=jax.ShapeDtypeStruct((block_count, BLK, lanes), F32),
        in_specs=[
            pl.BlockSpec(memory_space=pltpu.SMEM),
            pl.BlockSpec(rows.shape, lambda i: (0, 0)),
            piece,
            piece,
        ],
        out_specs=pl.BlockSpec((block_count, BLK, lanes), lambda i: (0, 0, 0)),
        compiler_params=pltpu.CompilerParams(vmem_limit_bytes=40 * 1024 * 1024),
    )(blocks, rows, own, other)
    return spread.reshape(spot_rows, lanes)


A_LAG, B_LAG, C_LAG, D_LAG, E_LAG = 1, 3, 5, 7, 8
PHASES = 2 * LEVELS - 1
ROOT = LEVELS - 1
MESH = pl.DeviceIdType.MESH


def level_of(phase):
    return phase if phase <= ROOT else 2 * ROOT - phase


def plan(bits, heights, tile):
    items, sums, busy = [], {}, 0
    ready = [0] * CHUNKS
    for phase in range(PHASES):
        count = heights[level_of(phase)] // tile
        for chunk in range(CHUNKS):
            start = max(busy, ready[chunk])
            busy = start + count
            items.append((start, count, phase, chunk))
            last = start + count - 1 + E_LAG
            target = phase + 1 if phase < ROOT else level_of(phase)
            step = 3 if bits[target] == 1 else 2
            sums[phase, chunk] = [last + step * j for j in range(bits[target] + 1)]
            ready[chunk] = sums[phase, chunk][-1] + 1
    end = max(ticks[-1] for ticks in sums.values()) + 1
    return items, sums, end


def solve_kernel(
    bits, heights, tile, z_count, first_ref, later_ref, row_live_ref, inner_live_ref, factor_ref, link_ref,
    out_ref, wide, core_land, in_land, mid_land, mine, theirs, sums_sent, held, make_w, make_g, use_w, use_g,
    acc, right, front_land, front_src, make_sem, use_sem, core_s, core_r, in_s, in_r, mid_s, mid_r,
    out_s, out_r, swap_s, swap_r, front_s, front_r,
):
    items, sums, end = plan(bits, heights, tile)
    counts = [height // tile for height in heights]
    most = max(counts)
    starts = [sum(counts[:level]) for level in range(LEVELS)]
    odd = max(counts[level_of(phase)] for phase in range(1, PHASES, 2))
    half = mine.shape[1]
    elem_at, front_at = lax.axis_index("elem"), lax.axis_index("front")
    z_at, core_at = elem_at // 2, elem_at % 2
    middle = z_count // 2
    low = (z_at < middle).astype(jnp.int32)
    depth = low * z_at + (1 - low) * (z_count - 1 - z_at)
    toward = 2 * low - 1
    is_outer, is_inner = depth == 0, depth == middle - 1
    sibling = {"elem": z_at * 2 + 1 - core_at}
    nearer = {"elem": (z_at + toward) * 2 + core_at}
    farther_at = (z_at - toward) * (depth > 0).astype(jnp.int32) + z_at * (depth == 0).astype(jnp.int32)
    farther = {"elem": farther_at * 2 + core_at}

    def partner(bit):
        low_part = front_at % (1 << bit)
        bit_now = front_at // (1 << bit) % 2
        high_part = front_at // (2 << bit) * (2 << bit)
        return {"front": high_part + (1 - bit_now) * (1 << bit) + low_part}

    all_bits = max(bits)
    barrier = pltpu.get_barrier_semaphore()

    def greet(device):
        pl.semaphore_signal(barrier, inc=1, device_id=device, device_id_type=MESH)

    greet(sibling)
    greet(nearer)
    for bit in range(all_bits):
        greet(partner(bit))
    pl.when(depth > 0)(lambda: greet(farther))
    pl.semaphore_wait(barrier, 2 + all_bits + (depth > 0).astype(jnp.int32))

    def decode(tick):
        valid = phase = chunk = sub = level = 0
        for start, count, phase_at, chunk_at in items:
            hit = jnp.logical_and(tick >= start, tick < start + count).astype(jnp.int32)
            valid += hit
            phase += hit * phase_at
            chunk += hit * chunk_at
            sub += hit * (tick - start)
            level += hit * starts[level_of(phase_at)]
        return valid == 1, phase, chunk, sub, level + sub

    def mid_slot(phase, chunk, sub):
        return chunk * (most + odd) + phase % 2 * most + sub

    def remote(source, target, send, receive, device):
        return pltpu.make_async_remote_copy(
            src_ref=source, dst_ref=target, send_sem=send, recv_sem=receive, device_id=device, device_id_type=MESH
        )

    def core_copy(tick, slot):
        return remote(theirs.at[tick % RING], core_land.at[slot], core_s.at[slot], core_r.at[slot], sibling)

    def in_copy(tick, slot):
        return remote(sums_sent.at[tick % HELD], in_land.at[slot], in_s.at[slot], in_r.at[slot], nearer)

    def mid_copy(tick, slot):
        return remote(sums_sent.at[tick % HELD], mid_land.at[slot], mid_s.at[slot], mid_r.at[slot], nearer)

    def out_copy(slot):
        place = wide.at[slot, pl.ds(0, half)]
        return remote(place, place, out_s.at[slot], out_r.at[slot], farther)

    def swap_copy(slot):
        return remote(
            wide.at[slot, pl.ds(0, half)], wide.at[slot, pl.ds(half, half)], swap_s.at[slot], swap_r.at[slot], sibling
        )

    def factor_copy(buffer, sem, ring, block):
        at = pl.multiple_of(block * tile, tile)
        return pltpu.make_async_copy(factor_ref.at[pl.ds(at, tile), :], buffer.at[ring], sem.at[ring])

    def link_copy(buffer, sem, ring, block):
        at = pl.multiple_of(block * tile, tile)
        return pltpu.make_async_copy(link_ref.at[:, pl.ds(at, tile)], buffer.at[ring], sem.at[ring])

    def make_load(tick, act):
        valid, phase, chunk, sub, block = decode(tick)
        ring = tick % RING
        pl.when(jnp.logical_and(valid, phase <= ROOT))(lambda: act(factor_copy(make_w, make_sem, ring, block)))
        pl.when(jnp.logical_and(valid, phase > ROOT))(lambda: act(link_copy(make_g, make_sem, ring, block)))

    def use_load(tick, act):
        valid, phase, chunk, sub, block = decode(tick)
        ring = (tick + RING) % RING
        pl.when(jnp.logical_and(valid, phase >= ROOT))(lambda: act(factor_copy(use_w, use_sem, ring, block)))
        pl.when(jnp.logical_and(valid, phase < ROOT))(lambda: act(link_copy(use_g, use_sem, ring, block)))

    def contract(left, right_value, axis):
        return lax.dot_general(left, right_value, (((1,), (axis,)), ((), ())), preferred_element_type=F32)

    for chunk in range(CHUNKS):
        right[chunk] = first_ref[chunk]

    def step_d(tick):
        valid, phase, chunk, sub, block = decode(tick)
        slot = chunk * most + sub

        @pl.when(jnp.logical_and(valid, jnp.logical_not(is_inner)))
        def _():
            out_copy(slot).wait_recv()
            swap_copy(slot).start()
            pl.when(depth > 0)(lambda: out_copy(slot).start())

    def step_c(tick):
        valid, phase, chunk, sub, block = decode(tick)
        slot = chunk * most + sub
        mid = mid_slot(phase, chunk, sub)
        kept = chunk * starts[ROOT] + block

        @pl.when(jnp.logical_and(valid, is_inner))
        def _():
            mid_copy(tick, mid).wait()
            total = sums_sent[tick % HELD].astype(F32) + mid_land[mid].astype(F32)
            live = row_live_ref[block]

            @pl.when(phase <= ROOT)
            def _():
                value = (live * total).astype(BF)
                wide[slot, pl.ds(0, half)] = value

                @pl.when(phase < ROOT)
                def _():
                    held[kept] = value

            @pl.when(phase > ROOT)
            def _():
                wide[slot, pl.ds(0, half)] = (live * (held[kept].astype(F32) - total)).astype(BF)

            swap_copy(slot).start()
            if middle > 1:
                out_copy(slot).start()

        if middle > 2:

            @pl.when(jnp.logical_and(valid, jnp.logical_and(depth > 0, jnp.logical_not(is_inner))))
            def _():
                in_copy(tick, slot).wait_send()

    def step_b(tick):
        valid, phase, chunk, sub, block = decode(tick)
        slot = chunk * most + sub

        if middle > 1:

            @pl.when(jnp.logical_and(valid, is_outer))
            def _():
                in_copy(tick, slot).wait_send()

            @pl.when(jnp.logical_and(valid, depth > 0))
            def _():
                in_copy(tick, slot).wait_recv()
                sums_sent[tick % HELD] = (mine[tick % HELD] + in_land[slot].astype(F32)).astype(BF)
                pl.when(is_inner)(lambda: mid_copy(tick, mid_slot(phase, chunk, sub)).start())
                if middle > 2:
                    pl.when(jnp.logical_not(is_inner))(lambda: in_copy(tick, slot).start())

    def step_a(tick):
        valid, phase, chunk, sub, block = decode(tick)
        slot = chunk * most + sub

        @pl.when(valid)
        def _():
            core_copy(tick, slot).wait()

            @pl.when(is_outer)
            def _():
                sums_sent[tick % HELD] = (mine[tick % HELD] + core_land[slot].astype(F32)).astype(BF)
                if middle > 1:
                    in_copy(tick, slot).start()
                else:
                    mid_copy(tick, mid_slot(phase, chunk, sub)).start()

            @pl.when(depth > 0)
            def _():
                mine[tick % HELD] = mine[tick % HELD] + core_land[slot].astype(F32)

    def step_e(tick):
        valid, phase, chunk, sub, block = decode(tick)
        slot = chunk * most + sub
        use_load(tick, lambda copy: copy.wait())

        @pl.when(valid)
        def _():
            swap_copy(slot).wait()
            pl.when(depth > 0)(lambda: out_copy(slot).wait_send())
            ring = tick % RING

            @pl.when(sub == 0)
            def _():
                acc[chunk] = jnp.zeros(acc.shape[1:], F32)

            @pl.when(phase < ROOT)
            def _():
                acc[chunk] += contract(wide[slot], use_g[ring], 1)

            @pl.when(phase >= ROOT)
            def _():
                acc[chunk] += contract(wide[slot], use_w[ring], 0)

    lands, land_at = {}, 0
    for phase in range(PHASES):
        target = phase + 1 if phase < ROOT else level_of(phase)
        for j in range(bits[target]):
            lands[phase, j] = land_at
            land_at += 1

    def front_copies(phase, j, target, chunk):
        count = bits[target]
        for part in range(2):
            bit = j if part == 0 else count - 1 - j
            rows = pl.ds(part * half, half)
            at = lands[phase, j] * CHUNKS + chunk
            yield remote(
                front_src.at[chunk, rows], front_land.at[at, rows], front_s.at[at * 2 + part],
                front_r.at[at * 2 + part], partner(bit),
            )

    def finish(tick):
        for phase in range(PHASES):
            target = phase + 1 if phase < ROOT else level_of(phase)
            ticks = [sums[phase, chunk] for chunk in range(CHUNKS)]
            for j in range(bits[target] + 1):
                now = [ticks[chunk][j] for chunk in range(CHUNKS)]
                hits = [tick == at for at in now]

                @pl.when(jnp.logical_or(*hits))
                def _(phase=phase, j=j, target=target, hits=hits):
                    chunk = hits[1].astype(jnp.int32)
                    value = acc[chunk]
                    if j == 0 and phase < ROOT:
                        value = later_ref[(target - 1) * CHUNKS + chunk].astype(F32) - value
                    if j:
                        for copy in front_copies(phase, j - 1, target, chunk):
                            copy.wait()
                        value = value + front_land[lands[phase, j - 1] * CHUNKS + chunk].astype(F32)
                    if j < bits[target]:
                        acc[chunk] = value
                        front_src[chunk] = value.astype(BF)
                        for copy in front_copies(phase, j, target, chunk):
                            copy.start()
                    else:
                        result = (inner_live_ref[target : target + 1, :] * value).astype(BF)
                        right[chunk] = result
                        if phase >= ROOT:
                            out_ref[target * CHUNKS + chunk] = result

    def step_make(tick):
        valid, phase, chunk, sub, block = decode(tick)
        slot = chunk * most + sub
        make_load(tick, lambda copy: copy.wait())

        @pl.when(valid)
        def _():
            ring = tick % RING

            def place(product):
                mine[tick % HELD] = product[:half]
                theirs[ring] = product[half:].astype(BF)

            @pl.when(phase <= ROOT)
            def _():
                place(contract(right[chunk], make_w[ring], 1))

            @pl.when(phase > ROOT)
            def _():
                place(contract(right[chunk], make_g[ring], 0))

            core_copy(tick, slot).start()

    ahead = RING - 1
    for tick in range(ahead):
        make_load(jnp.int32(tick), lambda copy: copy.start())

    def tick_body(tick, carry):
        make_load(tick + ahead, lambda copy: copy.start())
        use_load(tick - E_LAG + ahead, lambda copy: copy.start())
        step_d(tick - D_LAG)
        step_c(tick - C_LAG)
        step_b(tick - B_LAG)
        step_a(tick - A_LAG)
        step_e(tick - E_LAG)
        finish(tick)
        step_make(tick)
        return carry

    lax.fori_loop(0, end, tick_body, 0)


def solve(first, later, row_live, inner_live, factor, links, bits, heights, z_count):
    wide_columns, inner = first.shape[1:]
    half = wide_columns // 2
    tile = min(TILE, min(heights))
    counts = [height // tile for height in heights]
    most = max(counts)
    odd = max(counts[level_of(phase)] for phase in range(1, PHASES, 2))
    slots = CHUNKS * most
    mids = CHUNKS * (most + odd)
    lands = CHUNKS * sum(bits[phase + 1 if phase < ROOT else level_of(phase)] for phase in range(PHASES))
    kept = CHUNKS * sum(counts[:ROOT])
    lives = row_live.reshape(sum(counts), 1, tile)
    dma = pltpu.SemaphoreType.DMA
    vmem = pltpu.VMEM
    in_vmem, anywhere = pl.BlockSpec(memory_space=pltpu.VMEM), pl.BlockSpec(memory_space=pl.ANY)
    kernel = functools.partial(solve_kernel, bits, heights, tile, z_count)
    flops = 4 * wide_columns * CHUNKS * (factor.size + links.size)
    answers = pl.pallas_call(
        kernel,
        out_shape=jax.ShapeDtypeStruct((LEVELS * CHUNKS, wide_columns, inner), BF),
        in_specs=[in_vmem] * 4 + [anywhere] * 2,
        out_specs=in_vmem,
        scratch_shapes=[
            vmem((slots, wide_columns, tile), BF),
            vmem((slots, half, tile), BF),
            vmem((slots, half, tile), BF),
            vmem((mids, half, tile), BF),
            vmem((HELD, half, tile), F32),
            vmem((RING, half, tile), BF),
            vmem((HELD, half, tile), BF),
            vmem((kept, half, tile), BF),
            vmem((RING, tile, inner), BF),
            vmem((RING, inner, tile), BF),
            vmem((RING, tile, inner), BF),
            vmem((RING, inner, tile), BF),
            vmem((CHUNKS, wide_columns, inner), F32),
            vmem((CHUNKS, wide_columns, inner), BF),
            vmem((lands, wide_columns, inner), BF),
            vmem((CHUNKS, wide_columns, inner), BF),
            dma((RING,)),
            dma((RING,)),
            dma((slots,)),
            dma((slots,)),
            dma((slots,)),
            dma((slots,)),
            dma((mids,)),
            dma((mids,)),
            dma((slots,)),
            dma((slots,)),
            dma((slots,)),
            dma((slots,)),
            dma((2 * lands,)),
            dma((2 * lands,)),
        ],
        cost_estimate=pl.CostEstimate(flops=flops, bytes_accessed=8 * (factor.size + links.size), transcendentals=0),
        compiler_params=pltpu.CompilerParams(
            collective_id=0, has_side_effects=True, vmem_limit_bytes=63 * 1024 * 1024
        ),
    )(first, later, lives, inner_live, factor, links)
    return answers.reshape(LEVELS, CHUNKS, wide_columns, inner)


def body(
    elem_mat, elem_deriv, elem_disp, elem_sens, design_var, dof_rows, inverse_factor, coupling, front_sizes
):
    depth_bits = lax.axis_size("front").bit_length() - 1
    elem_count = lax.axis_size("elem")
    z_count = elem_count // 2
    device = lax.axis_index("front")
    elem_at = lax.axis_index("elem")
    z_at, core_at = elem_at // 2, elem_at % 2
    inner = coupling.shape[0]
    solve_size = inner * elem_count
    spot_rows = inverse_factor.shape[0]
    columns = elem_sens.shape[2]
    own_columns = columns // elem_count
    grain = own_columns // CHUNKS
    half = z_count * grain

    def core_swap(value):
        return lax.ppermute(value, "elem", [(i, i ^ 1) for i in range(elem_count)])

    def hop(value, pairs):
        steps = [(2 * a + c, 2 * b + c) for a, b in pairs for c in range(2)]
        return lax.ppermute(value, "elem", steps)

    def front_swap(value, bit):
        return lax.ppermute(value, "front", [(i, i ^ 1 << bit) for i in range(lax.axis_size("front"))])

    def in_group(value, share):
        count = lax.axis_size("front")
        groups = [list(range(i, i + share)) for i in range(0, count, share)]
        return lax.all_to_all(value, "front", split_axis=0, concat_axis=0, tiled=True, axis_index_groups=groups)

    facts = []
    offset = 0
    first_front = 0
    for level_at in range(LEVELS):
        bit_count = depth_bits - (LEVELS - 1 - level_at)
        block_rows = solve_size >> bit_count
        front_id = first_front + (device >> bit_count)
        size_now = lax.dynamic_index_in_dim(front_sizes, front_id, 0, keepdims=False)
        start = (device & (1 << bit_count) - 1) * block_rows
        row_live = (start + lax.iota(jnp.int32, block_rows) < size_now).astype(F32)[None, :]
        inner_live = (elem_at * inner + lax.iota(jnp.int32, inner) < size_now).astype(F32)[None, :]
        facts.append((bit_count, block_rows, offset, row_live, inner_live))
        offset = offset + block_rows
        first_front = first_front + (1 << LEVELS - 1 - level_at)

    place = lax.iota(jnp.int32, columns)
    place_core, rest = place // (z_count * own_columns), place % (z_count * own_columns)
    place_chunk, rest = rest // half, rest % half
    column_ids = (rest // grain * 2 + place_core) * own_columns + place_chunk * grain + rest % grain
    order = (place[:, None] == column_ids[None, :]).astype(BF)
    sens = jnp.einsum("ejc,cd->ejd", elem_sens, order, preferred_element_type=F32).astype(BF)

    pseudo = local_pseudo(elem_mat, elem_deriv, elem_disp, sens, design_var, column_ids).astype(BF)
    side = columns // 2
    own_pseudo = lax.dynamic_slice_in_dim(pseudo, core_at * side, side, 2)
    other_pseudo = core_swap(lax.dynamic_slice_in_dim(pseudo, (1 - core_at) * side, side, 2))
    places = jnp.concatenate([dof_rows, core_swap(dof_rows)], 1)
    blocks, rows = block_places(places, spot_rows)

    def chain_scatter(value):
        for s in range(z_count - 1):
            up, down = value[s + 1 :], value[: z_count - 1 - s]
            sent = jnp.where(z_at == s, up, down).astype(BF)
            got = hop(sent, [(s, s + 1), (z_count - 1 - s, z_count - 2 - s)]).astype(F32)
            is_up, is_down = z_at == s + 1, z_at == z_count - 2 - s
            gap = jnp.zeros((s + 1,) + value.shape[1:], F32)
            raised = jnp.where(is_up, jnp.concatenate([gap, got]), jnp.concatenate([got, gap]))
            value = value + jnp.where(is_up | is_down, raised, 0.0)
        return lax.dynamic_index_in_dim(value, z_at, 0, keepdims=False)

    given = [[None] * CHUNKS for _ in range(LEVELS)]

    def load_level(spread, pair_at, level_at):
        bit_count, block_rows, offset, row_live, inner_live = facts[level_at]
        piece = spread[offset : offset + block_rows]
        lanes = piece.shape[1]
        share = 1 << bit_count
        depth = inner // share
        if share > 1:
            piece = piece.reshape(elem_count // share, share, depth, lanes).swapaxes(0, 1)
            piece = in_group(piece.astype(BF), share).astype(F32)
        mine = chain_scatter(piece.reshape(z_count, 2 * depth, lanes)).astype(BF)
        own = lax.dynamic_slice_in_dim(mine, core_at * depth, depth, 0)
        other = core_swap(lax.dynamic_slice_in_dim(mine, (1 - core_at) * depth, depth, 0))
        both = jnp.concatenate([own.T.reshape(PAIR, half, depth), other.T.reshape(PAIR, half, depth)], 1)
        if share > 1:
            at = (device & share - 1) * depth
            both = lax.dynamic_update_slice_in_dim(jnp.zeros((PAIR, 2 * half, inner), BF), both, at, 2)
        for i in range(PAIR):
            given[level_at][pair_at * PAIR + i] = both[i]

    spreads = []
    for pair_at in range(CHUNKS // PAIR):
        spreads.append(scatter_rows(own_pseudo, other_pseudo, pair_at, blocks, rows, spot_rows))
        for level_at in range(LEVELS):
            load_level(spreads[pair_at], pair_at, level_at)

    def sum_group(value, bit_count):
        for bit_at in range(bit_count):
            value = value + front_swap(value.astype(BF), bit_at).astype(F32)
        return value

    first = [
        (facts[0][4] * sum_group(given[0][chunk].astype(F32), facts[0][0])).astype(BF) for chunk in range(CHUNKS)
    ]
    later = [given[level_at][chunk] for level_at in range(1, LEVELS) for chunk in range(CHUNKS)]
    row_live = jnp.concatenate([fact[3] for fact in facts], 1)
    inner_live = jnp.concatenate([fact[4] for fact in facts], 0)
    answers = solve(
        jnp.stack(first), jnp.stack(later), row_live, inner_live, inverse_factor, coupling,
        [fact[0] for fact in facts], [fact[1] for fact in facts], z_count,
    )

    def piece_of(level_at):
        bit_count, block_rows = facts[level_at][:2]
        share = 1 << bit_count
        depth = inner // share
        whole = answers[level_at]
        if share > 1:
            at = (device & share - 1) * depth
            whole = lax.dynamic_slice_in_dim(whole, at, depth, 2)
        own, other = whole[:, :half], core_swap(whole[:, half:])
        first = jnp.where(core_at == 0, own, other)
        second = jnp.where(core_at == 0, other, own)
        both = jnp.stack([first, second], 2).reshape(CHUNKS, z_count, grain, 2, depth)
        both = both.transpose(1, 0, 2, 3, 4)
        groups = [[2 * z + c for z in range(z_count)] for c in range(2)]
        turned = lax.all_to_all(both, "elem", split_axis=0, concat_axis=0, tiled=True, axis_index_groups=groups)
        turned = turned.reshape(z_count, own_columns, 2, depth).swapaxes(1, 2).reshape(elem_count, own_columns, depth)
        if share > 1:
            turned = in_group(turned.reshape(share, elem_count // share, own_columns, depth), share)
            turned = turned.swapaxes(0, 1)
            turned = turned.transpose(0, 1, 3, 2).reshape(block_rows, own_columns)
        else:
            turned = turned.transpose(0, 2, 1).reshape(block_rows, own_columns)
        return turned

    return jnp.concatenate([piece_of(level_at) for level_at in range(LEVELS)], 0).astype(F32)


def solution(mesh):
    return jax.shard_map(
        body,
        mesh=mesh,
        in_specs=(
            P(None, None, ("elem", "front")),
            P(None, None, ("elem", "front")),
            P(None, ("elem", "front")),
            P(("elem", "front"), None, None),
            P(("elem", "front")),
            P(None, ("elem", "front")),
            P("front", "elem"),
            P("elem", "front"),
            P(),
        ),
        out_specs=P("front", "elem"),
        check_vma=False,
    )
```

```python
import functools

import jax
import jax.numpy as jnp
from jax import lax
from jax.experimental import pallas as pl
from jax.experimental.pallas import tpu as pltpu
from jax.sharding import PartitionSpec as P

LEVELS = 3
CHUNKS = 2
TILE = 512
RING = 2
HELD = 4
SENT = 8
BLK = 128
GROUP = 8
BF, F32 = jnp.bfloat16, jnp.float32


def local_pseudo(tables, derivs, disps, sens, variables, column_ids):
    pseudo = -jnp.einsum("ije,ejc->eic", tables, sens, preferred_element_type=F32)
    drive_term = -jnp.einsum("ije,je->ei", derivs, disps, preferred_element_type=F32)
    hit_column = (column_ids[None, :] == variables[:, None]).astype(F32)
    return pseudo + drive_term[:, :, None] * hit_column[:, None, :]


def scatter_kernel(blocks_ref, rows_ref, own_ref, other_ref, out_ref, total):
    total[...] = jnp.zeros_like(total)
    count, dof = own_ref.shape[0], rows_ref.shape[1]

    for source_at, source_ref in enumerate((own_ref, other_ref)):

        def step(group_at, carry):
            first = pl.multiple_of(group_at * GROUP, GROUP)
            entry = pl.multiple_of(source_at * count + first, GROUP)
            rows = rows_ref[pl.ds(entry, GROUP), :]
            spread = []
            for at in range(GROUP):
                lanes = jnp.broadcast_to(rows[at : at + 1, :], (BLK, dof))
                hits = lax.broadcasted_iota(jnp.int32, (BLK, dof), 0) == lanes
                spread.append(
                    jnp.dot(hits.astype(F32).astype(BF), source_ref[first + at], preferred_element_type=F32)
                )
            for at in range(GROUP):
                block = blocks_ref[entry + at]
                total[block] = total[block] + spread[at]
            return carry

        lax.fori_loop(0, count // GROUP, step, 0)

    def turn(block, carry):
        at = pl.multiple_of(block * BLK, BLK)
        out_ref[0, :, pl.ds(at, BLK)] = total[block].T.astype(BF)
        return carry

    lax.fori_loop(0, total.shape[0], turn, 0)


def block_places(places, spot_rows):
    places = places.T
    used = places < spot_rows
    blocks = jnp.min(jnp.where(used, places, spot_rows), 1) // BLK
    blocks = jnp.clip(blocks, 0, spot_rows // BLK - 1)
    rows = jnp.where(used, places - blocks[:, None] * BLK, -1)
    return blocks, rows


def scatter_rows(own, other, blocks, rows, spot_rows):
    count, dof, width = own.shape
    lanes = width // CHUNKS
    piece = pl.BlockSpec((count, dof, lanes), lambda i: (0, 0, i))
    return pl.pallas_call(
        scatter_kernel,
        grid=(CHUNKS,),
        out_shape=jax.ShapeDtypeStruct((CHUNKS, lanes, spot_rows), BF),
        in_specs=[
            pl.BlockSpec(memory_space=pltpu.SMEM),
            pl.BlockSpec(rows.shape, lambda i: (0, 0)),
            piece,
            piece,
        ],
        out_specs=pl.BlockSpec((1, lanes, spot_rows), lambda i: (i, 0, 0)),
        scratch_shapes=[pltpu.VMEM((spot_rows // BLK, BLK, lanes), F32)],
        compiler_params=pltpu.CompilerParams(vmem_limit_bytes=40 * 1024 * 1024),
    )(blocks, rows, own, other)


A_LAG, B_LAG, C_LAG, D_LAG, E_LAG = 1, 3, 5, 7, 8
PHASES = 2 * LEVELS - 1
ROOT = LEVELS - 1
MESH = pl.DeviceIdType.MESH


def level_of(phase):
    return phase if phase <= ROOT else 2 * ROOT - phase


def target_of(phase):
    return phase + 1 if phase < ROOT else level_of(phase)


def plan(bits, heights, tile, z_count):
    counts = [height // tile for height in heights]
    loads, items, sums, busy, load_busy = [], [], {}, 0, 0
    ready = [0] * CHUNKS

    def add_load(level, chunk, wanted):
        nonlocal load_busy
        count = (counts[level] + 1) // 2
        start = max(load_busy, wanted - count + 1 - 2 * z_count)
        load_busy = start + count
        loads.append((start, count, level, chunk))
        return load_busy - 1 + 2 * z_count

    def add_sum(phase, chunk, last):
        depth = bits[target_of(phase)]
        step = 3 if depth == 1 else 2
        sums[phase, chunk] = [last + step * j for j in range(depth + 1)]
        ready[chunk] = sums[phase, chunk][-1] + 1

    for chunk in range(CHUNKS):
        add_sum(-1, chunk, add_load(0, chunk, 0))
    for phase in range(PHASES):
        count = counts[level_of(phase)]
        for chunk in range(CHUNKS):
            start = max(busy, ready[chunk])
            busy = start + count
            items.append((start, count, phase, chunk))
            last = start + count - 1 + E_LAG
            if phase < ROOT:
                last = max(last, add_load(phase + 1, chunk, last))
            add_sum(phase, chunk, last)
    end = max(max(ticks[-1] for ticks in sums.values()), load_busy + 2 * z_count) + 1
    return loads, items, sums, end


def solve_kernel(
    bits, heights, tile, z_count, row_live_ref, inner_live_ref, load_ref, factor_ref, link_ref,
    out_ref, wide, core_land, in_land, mid_land, mine, theirs, sums_sent, held, make_w, make_g, use_w, use_g,
    acc, right, front_land, front_src, given, term, make_sem, use_sem, core_s, core_r, in_s, in_r, mid_s, mid_r,
    out_s, out_r, swap_s, swap_r, front_s, front_r, term_sem, term_s, up_r, down_r, given_r, end_s, end_r,
):
    loads, items, sums, end = plan(bits, heights, tile, z_count)
    counts = [height // tile for height in heights]
    most = max(counts)
    starts = [sum(counts[:level]) for level in range(LEVELS)]
    odd = max(counts[level_of(phase)] for phase in range(1, PHASES, 2))
    half = mine.shape[1]
    elem_at, front_at = lax.axis_index("elem"), lax.axis_index("front")
    z_at, core_at = elem_at // 2, elem_at % 2
    middle = z_count // 2
    low = (z_at < middle).astype(jnp.int32)
    depth = low * z_at + (1 - low) * (z_count - 1 - z_at)
    toward = 2 * low - 1
    is_outer, is_inner = depth == 0, depth == middle - 1
    sibling = {"elem": z_at * 2 + 1 - core_at}
    nearer = {"elem": (z_at + toward) * 2 + core_at}
    farther_at = (z_at - toward) * (depth > 0).astype(jnp.int32) + z_at * (depth == 0).astype(jnp.int32)
    farther = {"elem": farther_at * 2 + core_at}

    def partner(bit):
        low_part = front_at % (1 << bit)
        bit_now = front_at // (1 << bit) % 2
        high_part = front_at // (2 << bit) * (2 << bit)
        return {"front": high_part + (1 - bit_now) * (1 << bit) + low_part}

    elem_count = 2 * z_count
    inner = given.shape[2]
    per = inner // tile
    grain = half // z_count
    first_tile = [front_at % (1 << bits[level]) * counts[level] for level in range(LEVELS)]
    own_tile = elem_at * per

    def owns(level):
        return jnp.logical_and(own_tile >= first_tile[level], own_tile < first_tile[level] + counts[level])

    given[...] = jnp.zeros_like(given)
    all_bits = max(bits)
    barrier = pltpu.get_barrier_semaphore()

    def greet(device):
        pl.semaphore_signal(barrier, inc=1, device_id=device, device_id_type=MESH)

    for shift in range(1, elem_count):
        greet({"elem": (elem_at + shift) % elem_count})
    for bit in range(all_bits):
        greet(partner(bit))
    pl.semaphore_wait(barrier, elem_count - 1 + all_bits)

    def decode(tick):
        valid = phase = chunk = sub = level = 0
        for start, count, phase_at, chunk_at in items:
            hit = jnp.logical_and(tick >= start, tick < start + count).astype(jnp.int32)
            valid += hit
            phase += hit * phase_at
            chunk += hit * chunk_at
            sub += hit * (tick - start)
            level += hit * starts[level_of(phase_at)]
        return valid == 1, phase, chunk, sub, level + sub

    def mid_slot(phase, chunk, sub):
        return chunk * (most + odd) + phase % 2 * most + sub

    def remote(source, target, send, receive, device):
        return pltpu.make_async_remote_copy(
            src_ref=source, dst_ref=target, send_sem=send, recv_sem=receive, device_id=device, device_id_type=MESH
        )

    def core_copy(tick, slot):
        return remote(theirs.at[tick % RING], core_land.at[slot], core_s.at[slot], core_r.at[slot], sibling)

    def in_copy(tick, slot):
        return remote(sums_sent.at[tick % SENT], in_land.at[slot], in_s.at[slot], in_r.at[slot], nearer)

    def mid_copy(tick, slot):
        return remote(sums_sent.at[tick % SENT], mid_land.at[slot], mid_s.at[slot], mid_r.at[slot], nearer)

    def out_copy(slot):
        place = wide.at[slot, pl.ds(0, half)]
        return remote(place, place, out_s.at[slot], out_r.at[slot], farther)

    def swap_copy(slot):
        return remote(
            wide.at[slot, pl.ds(0, half)], wide.at[slot, pl.ds(half, half)], swap_s.at[slot], swap_r.at[slot], sibling
        )

    def factor_copy(buffer, sem, ring, block):
        at = pl.multiple_of(block * tile, tile)
        return pltpu.make_async_copy(factor_ref.at[pl.ds(at, tile), :], buffer.at[ring], sem.at[ring])

    def link_copy(buffer, sem, ring, block):
        at = pl.multiple_of(block * tile, tile)
        return pltpu.make_async_copy(link_ref.at[:, pl.ds(at, tile)], buffer.at[ring], sem.at[ring])

    def make_load(tick, act):
        valid, phase, chunk, sub, block = decode(tick)
        ring = tick % RING
        pl.when(jnp.logical_and(valid, phase <= ROOT))(lambda: act(factor_copy(make_w, make_sem, ring, block)))
        pl.when(jnp.logical_and(valid, phase > ROOT))(lambda: act(link_copy(make_g, make_sem, ring, block)))

    def use_load(tick, act):
        valid, phase, chunk, sub, block = decode(tick)
        ring = (tick + E_LAG) % RING
        pl.when(jnp.logical_and(valid, phase >= ROOT))(lambda: act(factor_copy(use_w, use_sem, ring, block)))
        pl.when(jnp.logical_and(valid, phase < ROOT))(lambda: act(link_copy(use_g, use_sem, ring, block)))

    def contract(left, right_value, axis):
        return lax.dot_general(left, right_value, (((1,), (axis,)), ((), ())), preferred_element_type=F32)

    span = 2 * z_count
    rest = sum(counts[1:])

    def decode_load(tick):
        valid = chunk = at = count = origin = block = slot = kept = 0
        for start, pairs, level, chunk_at in loads:
            hit = jnp.logical_and(tick >= start, tick < start + pairs).astype(jnp.int32)
            valid += hit
            chunk += hit * chunk_at
            at += hit * (tick - start)
            count += hit * counts[level]
            origin += hit * first_tile[level]
            block += hit * starts[level]
            base = chunk_at * most if level == 0 else CHUNKS * most + chunk_at * rest + starts[level] - counts[0]
            slot += hit * base
            kept += hit * (level * CHUNKS + chunk_at)
        tiles = []
        for which in range(2):
            tile_at = at if which == 0 else count - 1 - at
            there = valid == 1 if which == 0 else jnp.logical_and(valid == 1, tile_at > at)
            owner = (origin + tile_at) // per
            sub = (origin + tile_at) % per
            ring = (tick + span) % span * 2 + which
            tiles.append((there, chunk, block + tile_at, slot + tile_at, kept, owner // 2, owner % 2, sub, ring))
        return tiles

    def term_copy(chunk, block, ring):
        at = pl.multiple_of(block * tile, tile)
        return pltpu.make_async_copy(load_ref.at[chunk, :, pl.ds(at, tile)], term.at[ring], term_sem.at[ring])

    upper = {"elem": (z_at + 1) % z_count * 2 + core_at}
    lower = {"elem": (z_at + z_count - 1) % z_count * 2 + core_at}

    def up_copy(ring, slot):
        return remote(term.at[ring], wide.at[slot, pl.ds(0, half)], term_s.at[ring], up_r.at[slot], upper)

    def down_copy(ring, slot):
        return remote(term.at[ring], wide.at[slot, pl.ds(half, half)], term_s.at[ring], down_r.at[slot], lower)

    def given_copy(ring, kept, sub):
        at = pl.multiple_of(sub * tile, tile)
        return remote(
            term.at[ring], given.at[kept, pl.ds(half, half), pl.ds(at, tile)], term_s.at[ring],
            given_r.at[kept * per + sub], sibling,
        )

    def load_retire(tick):
        for there, chunk, block, slot, kept, z_own, core_own, sub, ring in decode_load(tick):
            stays = jnp.logical_and(z_own == z_at, core_own == core_at)
            pl.when(jnp.logical_and(there, jnp.logical_not(stays)))(lambda ring=ring, slot=slot: up_copy(ring, slot).wait_send())

    def load_start(tick):
        for there, chunk, block, slot, kept, z_own, core_own, sub, ring in decode_load(tick):
            pl.when(there)(lambda chunk=chunk, block=block, ring=ring: term_copy(chunk, block, ring).start())

    def load_stage(tick, stage):
        for there, chunk, block, slot, kept, z_own, core_own, sub, ring in decode_load(tick):
            rises = jnp.logical_and(there, jnp.logical_and(z_at < z_own, z_at == stage))
            falls = jnp.logical_and(there, jnp.logical_and(z_at > z_own, z_count - 1 - z_at == stage))
            if stage < z_count - 1:

                @pl.when(rises)
                def _(chunk=chunk, block=block, slot=slot, ring=ring):
                    term_copy(chunk, block, ring).wait()
                    if stage:
                        up_copy(ring, slot).wait_recv()
                        total = term[ring].astype(F32) + wide[slot, pl.ds(0, half)].astype(F32)
                        term[ring] = total.astype(BF)
                    up_copy(ring, slot).start()

                @pl.when(falls)
                def _(chunk=chunk, block=block, slot=slot, ring=ring):
                    term_copy(chunk, block, ring).wait()
                    if stage:
                        down_copy(ring, slot).wait_recv()
                        total = term[ring].astype(F32) + wide[slot, pl.ds(half, half)].astype(F32)
                        term[ring] = total.astype(BF)
                    down_copy(ring, slot).start()

            else:

                @pl.when(jnp.logical_and(there, z_at == z_own))
                def _(chunk=chunk, block=block, slot=slot, kept=kept, core_own=core_own, sub=sub, ring=ring):
                    term_copy(chunk, block, ring).wait()

                    @pl.when(z_at > 0)
                    def _():
                        up_copy(ring, slot).wait_recv()
                        total = term[ring].astype(F32) + wide[slot, pl.ds(0, half)].astype(F32)
                        term[ring] = total.astype(BF)

                    @pl.when(z_at < z_count - 1)
                    def _():
                        down_copy(ring, slot).wait_recv()
                        total = term[ring].astype(F32) + wide[slot, pl.ds(half, half)].astype(F32)
                        term[ring] = total.astype(BF)

                    @pl.when(core_own == core_at)
                    def _():
                        at = pl.multiple_of(sub * tile, tile)
                        given[kept, pl.ds(0, half), pl.ds(at, tile)] = term[ring]

                    @pl.when(core_own != core_at)
                    def _():
                        given_copy(ring, kept, sub).start()

    offsets = [starts[level] * tile for level in range(LEVELS)]

    def end_copy(level, chunk, place, side, z_to, sender):
        kept = level * CHUNKS + chunk
        at = pl.multiple_of(offsets[level] + (sender * per - first_tile[level]) * tile, tile)
        core_to = core_at if side == 0 else 1 - core_at
        return remote(
            given.at[kept, pl.ds(side * half + z_to * grain, grain)],
            out_ref.at[pl.ds(pl.multiple_of(chunk * grain, grain), grain), pl.ds(at, inner)],
            end_s.at[kept * elem_count + z_to * 2 + side], end_r.at[kept * elem_count + sender],
            {"elem": z_to * 2 + core_to},
        )

    def end_sends(level, chunk, act):
        for z_to in range(z_count):
            for side in range(2):
                copy = end_copy(level, chunk, None, side, z_to, elem_at)
                if side:
                    act(copy)
                else:
                    pl.when(z_at != z_to)(lambda copy=copy: act(copy))

    def end_keep(level, chunk):
        kept = level * CHUNKS + chunk
        at = pl.multiple_of(offsets[level] + (own_tile - first_tile[level]) * tile, tile)
        rows = pl.ds(pl.multiple_of(chunk * grain, grain), grain)
        out_ref[rows, pl.ds(at, inner)] = given[kept, pl.ds(pl.multiple_of(z_at * grain, grain), grain), :]

    def end_waits():
        for level in range(LEVELS):
            for chunk in range(CHUNKS):
                pl.when(owns(level))(lambda: end_sends(level, chunk, lambda copy: copy.wait_send()))
                for sender in range(elem_count):
                    there = jnp.logical_and(
                        sender * per >= first_tile[level], sender * per < first_tile[level] + counts[level]
                    )

                    @pl.when(jnp.logical_and(there, elem_at != sender))
                    def _():
                        end_copy(level, chunk, None, 1, 0, sender).wait_recv()

    def step_d(tick):
        valid, phase, chunk, sub, block = decode(tick)
        slot = chunk * most + sub

        @pl.when(jnp.logical_and(valid, jnp.logical_not(is_inner)))
        def _():
            out_copy(slot).wait_recv()
            swap_copy(slot).start()
            pl.when(depth > 0)(lambda: out_copy(slot).start())

    def step_c(tick):
        valid, phase, chunk, sub, block = decode(tick)
        slot = chunk * most + sub
        mid = mid_slot(phase, chunk, sub)
        kept = chunk * starts[ROOT] + block

        @pl.when(jnp.logical_and(valid, is_inner))
        def _():
            mid_copy(tick, mid).wait()
            total = sums_sent[tick % SENT].astype(F32) + mid_land[mid].astype(F32)
            live = row_live_ref[block]

            @pl.when(phase <= ROOT)
            def _():
                value = (live * total).astype(BF)
                wide[slot, pl.ds(0, half)] = value

                @pl.when(phase < ROOT)
                def _():
                    held[kept] = value

            @pl.when(phase > ROOT)
            def _():
                wide[slot, pl.ds(0, half)] = (live * (held[kept].astype(F32) - total)).astype(BF)

            swap_copy(slot).start()
            if middle > 1:
                out_copy(slot).start()

        if middle > 2:

            @pl.when(jnp.logical_and(valid, jnp.logical_and(depth > 0, jnp.logical_not(is_inner))))
            def _():
                in_copy(tick, slot).wait_send()

    def step_b(tick):
        valid, phase, chunk, sub, block = decode(tick)
        slot = chunk * most + sub

        if middle > 1:

            @pl.when(jnp.logical_and(valid, is_outer))
            def _():
                in_copy(tick, slot).wait_send()

            @pl.when(jnp.logical_and(valid, depth > 0))
            def _():
                in_copy(tick, slot).wait_recv()
                sums_sent[tick % SENT] = (mine[tick % HELD] + in_land[slot].astype(F32)).astype(BF)
                pl.when(is_inner)(lambda: mid_copy(tick, mid_slot(phase, chunk, sub)).start())
                if middle > 2:
                    pl.when(jnp.logical_not(is_inner))(lambda: in_copy(tick, slot).start())

    def step_a(tick):
        valid, phase, chunk, sub, block = decode(tick)
        slot = chunk * most + sub

        @pl.when(valid)
        def _():
            core_copy(tick, slot).wait()

            @pl.when(is_outer)
            def _():
                sums_sent[tick % SENT] = (mine[tick % HELD] + core_land[slot].astype(F32)).astype(BF)
                if middle > 1:
                    in_copy(tick, slot).start()
                else:
                    mid_copy(tick, mid_slot(phase, chunk, sub)).start()

            @pl.when(depth > 0)
            def _():
                mine[tick % HELD] = mine[tick % HELD] + core_land[slot].astype(F32)

    def step_e(tick):
        valid, phase, chunk, sub, block = decode(tick)
        slot = chunk * most + sub
        use_load(tick, lambda copy: copy.wait())

        @pl.when(valid)
        def _():
            swap_copy(slot).wait()
            pl.when(depth > 0)(lambda: out_copy(slot).wait_send())
            ring = (tick + E_LAG) % RING

            @pl.when(sub == 0)
            def _():
                acc[chunk] = jnp.zeros(acc.shape[1:], F32)

            @pl.when(phase < ROOT)
            def _():
                acc[chunk] += contract(wide[slot], use_g[ring], 1)

            @pl.when(phase >= ROOT)
            def _():
                acc[chunk] += contract(wide[slot], use_w[ring], 0)

    lands, land_at = {}, 0
    for phase in range(-1, PHASES):
        for j in range(bits[target_of(phase)]):
            lands[phase, j] = land_at
            land_at += 1

    def front_copies(phase, j, target, chunk):
        count = bits[target]
        for part in range(2):
            bit = j if part == 0 else count - 1 - j
            rows = pl.ds(part * half, half)
            at = lands[phase, j] * CHUNKS + chunk
            yield remote(
                front_src.at[chunk, rows], front_land.at[at, rows], front_s.at[at * 2 + part],
                front_r.at[at * 2 + part], partner(bit),
            )

    def finish(tick):
        for phase in range(-1, PHASES):
            target = target_of(phase)
            ticks = [sums[phase, chunk] for chunk in range(CHUNKS)]
            for j in range(bits[target] + 1):
                hits = [tick == ticks[chunk][j] for chunk in range(CHUNKS)]

                @pl.when(jnp.logical_or(*hits))
                def _(phase=phase, j=j, target=target, hits=hits):
                    chunk = hits[1].astype(jnp.int32)
                    kept = target * CHUNKS + chunk
                    if j == 0 and phase < ROOT:

                        @pl.when(owns(target))
                        def _():
                            for sub in range(per):
                                given_copy(0, kept, sub).wait_recv()

                        value = given[kept].astype(F32)
                        if phase >= 0:
                            value = value - acc[chunk]
                    else:
                        value = acc[chunk]
                    if j:
                        for copy in front_copies(phase, j - 1, target, chunk):
                            copy.wait()
                        value = value + front_land[lands[phase, j - 1] * CHUNKS + chunk].astype(F32)
                    if j < bits[target]:
                        acc[chunk] = value
                        front_src[chunk] = value.astype(BF)
                        for copy in front_copies(phase, j, target, chunk):
                            copy.start()
                    else:
                        result = (inner_live_ref[target : target + 1, :] * value).astype(BF)
                        right[chunk] = result
                        if phase >= ROOT:
                            given[kept] = result

                            @pl.when(owns(target))
                            def _():
                                end_sends(target, chunk, lambda copy: copy.start())
                                end_keep(target, chunk)

    def step_make(tick):
        valid, phase, chunk, sub, block = decode(tick)
        slot = chunk * most + sub
        make_load(tick, lambda copy: copy.wait())

        @pl.when(valid)
        def _():
            ring = tick % RING

            def place(product):
                mine[tick % HELD] = product[:half]
                theirs[ring] = product[half:].astype(BF)

            @pl.when(phase <= ROOT)
            def _():
                place(contract(right[chunk], make_w[ring], 1))

            @pl.when(phase > ROOT)
            def _():
                place(contract(right[chunk], make_g[ring], 0))

            core_copy(tick, slot).start()

    ahead = RING - 1
    for tick in range(ahead):
        make_load(jnp.int32(tick), lambda copy: copy.start())

    def tick_body(tick, carry):
        make_load(tick + ahead, lambda copy: copy.start())
        use_load(tick - E_LAG + ahead, lambda copy: copy.start())
        load_retire(tick - span)
        load_start(tick)
        for stage in range(z_count):
            load_stage(tick - 1 - 2 * stage, stage)
        step_d(tick - D_LAG)
        step_c(tick - C_LAG)
        step_b(tick - B_LAG)
        step_a(tick - A_LAG)
        step_e(tick - E_LAG)
        finish(tick)
        step_make(tick)
        return carry

    lax.fori_loop(0, end, tick_body, 0)
    end_waits()


def solve(loads, row_live, inner_live, factor, links, bits, heights, z_count):
    half, inner = loads.shape[1], links.shape[0]
    wide_columns = 2 * half
    tile = min(TILE, min(heights))
    counts = [height // tile for height in heights]
    most = max(counts)
    odd = max(counts[level_of(phase)] for phase in range(1, PHASES, 2))
    slots = CHUNKS * most
    load_slots = CHUNKS * sum(counts)
    mids = CHUNKS * (most + odd)
    lands = CHUNKS * sum(bits[target_of(phase)] for phase in range(-1, PHASES))
    kept = CHUNKS * sum(counts[:ROOT])
    ends = LEVELS * CHUNKS * 2 * z_count
    lives = row_live.reshape(sum(counts), 1, tile)
    dma = pltpu.SemaphoreType.DMA
    vmem = pltpu.VMEM
    in_vmem, anywhere = pl.BlockSpec(memory_space=pltpu.VMEM), pl.BlockSpec(memory_space=pl.ANY)
    kernel = functools.partial(solve_kernel, bits, heights, tile, z_count)
    flops = 4 * wide_columns * CHUNKS * (factor.size + links.size)
    return pl.pallas_call(
        kernel,
        out_shape=jax.ShapeDtypeStruct((CHUNKS * half // z_count, factor.shape[0]), BF),
        in_specs=[in_vmem] * 2 + [anywhere] * 3,
        out_specs=in_vmem,
        scratch_shapes=[
            vmem((load_slots, wide_columns, tile), BF),
            vmem((slots, half, tile), BF),
            vmem((slots, half, tile), BF),
            vmem((mids, half, tile), BF),
            vmem((HELD, half, tile), F32),
            vmem((RING, half, tile), BF),
            vmem((SENT, half, tile), BF),
            vmem((kept, half, tile), BF),
            vmem((RING, tile, inner), BF),
            vmem((RING, inner, tile), BF),
            vmem((RING, tile, inner), BF),
            vmem((RING, inner, tile), BF),
            vmem((CHUNKS, wide_columns, inner), F32),
            vmem((CHUNKS, wide_columns, inner), BF),
            vmem((lands, wide_columns, inner), BF),
            vmem((CHUNKS, wide_columns, inner), BF),
            vmem((LEVELS * CHUNKS, wide_columns, inner), BF),
            vmem((4 * z_count, half, tile), BF),
            dma((RING,)),
            dma((RING,)),
            dma((slots,)),
            dma((slots,)),
            dma((slots,)),
            dma((slots,)),
            dma((mids,)),
            dma((mids,)),
            dma((slots,)),
            dma((slots,)),
            dma((slots,)),
            dma((slots,)),
            dma((2 * lands,)),
            dma((2 * lands,)),
            dma((4 * z_count,)),
            dma((4 * z_count,)),
            dma((load_slots,)),
            dma((load_slots,)),
            dma((LEVELS * CHUNKS * (inner // tile),)),
            dma((ends,)),
            dma((ends,)),
        ],
        cost_estimate=pl.CostEstimate(flops=flops, bytes_accessed=8 * (factor.size + links.size), transcendentals=0),
        compiler_params=pltpu.CompilerParams(
            collective_id=0, has_side_effects=True, vmem_limit_bytes=63 * 1024 * 1024
        ),
    )(lives, inner_live, loads, factor, links)


def body(
    elem_mat, elem_deriv, elem_disp, elem_sens, design_var, dof_rows, inverse_factor, coupling, front_sizes
):
    depth_bits = lax.axis_size("front").bit_length() - 1
    elem_count = lax.axis_size("elem")
    z_count = elem_count // 2
    device = lax.axis_index("front")
    elem_at = lax.axis_index("elem")
    z_at, core_at = elem_at // 2, elem_at % 2
    inner = coupling.shape[0]
    solve_size = inner * elem_count
    spot_rows = inverse_factor.shape[0]
    columns = elem_sens.shape[2]
    own_columns = columns // elem_count
    grain = own_columns // CHUNKS
    half = z_count * grain

    def core_swap(value):
        return lax.ppermute(value, "elem", [(i, i ^ 1) for i in range(elem_count)])

    facts = []
    offset = 0
    first_front = 0
    for level_at in range(LEVELS):
        bit_count = depth_bits - (LEVELS - 1 - level_at)
        block_rows = solve_size >> bit_count
        front_id = first_front + (device >> bit_count)
        size_now = lax.dynamic_index_in_dim(front_sizes, front_id, 0, keepdims=False)
        start = (device & (1 << bit_count) - 1) * block_rows
        row_live = (start + lax.iota(jnp.int32, block_rows) < size_now).astype(F32)[None, :]
        inner_live = (elem_at * inner + lax.iota(jnp.int32, inner) < size_now).astype(F32)[None, :]
        facts.append((bit_count, block_rows, offset, row_live, inner_live))
        offset = offset + block_rows
        first_front = first_front + (1 << LEVELS - 1 - level_at)

    place = lax.iota(jnp.int32, columns)
    place_core, rest = place // (z_count * own_columns), place % (z_count * own_columns)
    place_chunk, rest = rest // half, rest % half
    column_ids = (rest // grain * 2 + place_core) * own_columns + place_chunk * grain + rest % grain
    order = (place[:, None] == column_ids[None, :]).astype(BF)
    sens = jnp.einsum("ejc,cd->ejd", elem_sens, order, preferred_element_type=F32).astype(BF)

    pseudo = local_pseudo(elem_mat, elem_deriv, elem_disp, sens, design_var, column_ids).astype(BF)
    side = columns // 2
    own_pseudo = lax.dynamic_slice_in_dim(pseudo, core_at * side, side, 2)
    other_pseudo = core_swap(lax.dynamic_slice_in_dim(pseudo, (1 - core_at) * side, side, 2))
    places = jnp.concatenate([dof_rows, core_swap(dof_rows)], 1)
    blocks, rows = block_places(places, spot_rows)

    loads = scatter_rows(own_pseudo, other_pseudo, blocks, rows, spot_rows)
    row_live = jnp.concatenate([fact[3] for fact in facts], 1)
    inner_live = jnp.concatenate([fact[4] for fact in facts], 0)
    bits, heights = [fact[0] for fact in facts], [fact[1] for fact in facts]
    answers = solve(loads, row_live, inner_live, inverse_factor, coupling, bits, heights, z_count)
    return answers.astype(F32).T


def solution(mesh):
    return jax.shard_map(
        body,
        mesh=mesh,
        in_specs=(
            P(None, None, ("elem", "front")),
            P(None, None, ("elem", "front")),
            P(None, ("elem", "front")),
            P(("elem", "front"), None, None),
            P(("elem", "front")),
            P(None, ("elem", "front")),
            P("front", "elem"),
            P("elem", "front"),
            P(),
        ),
        out_specs=P("front", "elem"),
        check_vma=False,
    )
```

```python
import functools

import jax
import jax.numpy as jnp
from jax import lax
from jax.experimental import pallas as pl
from jax.experimental.pallas import tpu as pltpu
from jax.sharding import PartitionSpec as P

LEVELS = 3
CHUNKS = 2
TILE = 512
RING = 2
HELD = 4
SENT = 8
TURN = 512
SEND_GAP = 3
LOAD_LAG = 2
BLK = 128
GROUP = 8
BF, F32 = jnp.bfloat16, jnp.float32


def local_pseudo(tables, derivs, disps, sens, variables, column_ids):
    pseudo = -jnp.einsum("ije,ejc->eic", tables, sens, preferred_element_type=F32)
    drive_term = -jnp.einsum("ije,je->ei", derivs, disps, preferred_element_type=F32)
    hit_column = (column_ids[None, :] == variables[:, None]).astype(F32)
    return pseudo + drive_term[:, :, None] * hit_column[:, None, :]


def scatter_kernel(blocks_ref, rows_ref, own_ref, other_ref, out_ref, total):
    total[...] = jnp.zeros_like(total)
    count, dof = own_ref.shape[0], rows_ref.shape[1]

    for source_at, source_ref in enumerate((own_ref, other_ref)):

        def step(group_at, carry):
            first = pl.multiple_of(group_at * GROUP, GROUP)
            entry = pl.multiple_of(source_at * count + first, GROUP)
            rows = rows_ref[pl.ds(entry, GROUP), :]
            spread = []
            for at in range(GROUP):
                lanes = jnp.broadcast_to(rows[at : at + 1, :], (BLK, dof))
                hits = lax.broadcasted_iota(jnp.int32, (BLK, dof), 0) == lanes
                spread.append(
                    jnp.dot(hits.astype(F32).astype(BF), source_ref[first + at], preferred_element_type=F32)
                )
            for at in range(GROUP):
                block = blocks_ref[entry + at]
                total[block] = total[block] + spread[at]
            return carry

        lax.fori_loop(0, count // GROUP, step, 0)

    lanes = total.shape[2]
    same = lax.broadcasted_iota(jnp.int32, (lanes, lanes), 0) == lax.broadcasted_iota(jnp.int32, (lanes, lanes), 1)
    unit = same.astype(F32).astype(BF)
    turned = TURN // BLK
    width = lanes // CHUNKS

    def turn(step, carry):
        at = pl.multiple_of(step * TURN, TURN)
        piece = total[pl.ds(step * turned, turned)].reshape(TURN, lanes).astype(BF)
        moved = lax.dot_general(unit, piece, (((1,), (1,)), ((), ())), preferred_element_type=F32).astype(BF)
        for chunk in range(CHUNKS):
            out_ref[chunk, :, pl.ds(at, TURN)] = moved[chunk * width : (chunk + 1) * width]
        return carry

    lax.fori_loop(0, total.shape[0] // turned, turn, 0)


def block_places(places, spot_rows):
    places = places.T
    used = places < spot_rows
    blocks = jnp.min(jnp.where(used, places, spot_rows), 1) // BLK
    blocks = jnp.clip(blocks, 0, spot_rows // BLK - 1)
    rows = jnp.where(used, places - blocks[:, None] * BLK, -1)
    return blocks, rows


def scatter_rows(own, other, blocks, rows, spot_rows):
    width = own.shape[2]
    vmem = pl.BlockSpec(memory_space=pltpu.VMEM)
    return pl.pallas_call(
        scatter_kernel,
        out_shape=jax.ShapeDtypeStruct((CHUNKS, width // CHUNKS, spot_rows), BF),
        in_specs=[pl.BlockSpec(memory_space=pltpu.SMEM), vmem, vmem, vmem],
        out_specs=vmem,
        scratch_shapes=[pltpu.VMEM((spot_rows // BLK, BLK, width), F32)],
        compiler_params=pltpu.CompilerParams(vmem_limit_bytes=40 * 1024 * 1024),
    )(blocks, rows, own, other)


A_LAG, B_LAG, C_LAG, D_LAG, E_LAG = 1, 3, 5, 7, 8
PHASES = 2 * LEVELS - 1
ROOT = LEVELS - 1
MESH = pl.DeviceIdType.MESH


def level_of(phase):
    return phase if phase <= ROOT else 2 * ROOT - phase


def target_of(phase):
    return phase + 1 if phase < ROOT else level_of(phase)


def plan(bits, heights, tile, z_count):
    counts = [height // tile for height in heights]
    loads, items, sums, busy, load_busy = [], [], {}, 0, 0
    ready = [0] * CHUNKS

    def add_load(level, chunk, wanted):
        nonlocal load_busy
        count = (counts[level] + 1) // 2
        start = max(load_busy, wanted - count - 1 - LOAD_LAG * (z_count - 1))
        load_busy = start + count
        loads.append((start, count, level, chunk))
        return load_busy - 1 + LOAD_LAG * (z_count - 1) + 2

    def add_sum(phase, chunk, last):
        depth = bits[target_of(phase)]
        step = 3 if depth == 1 else 2
        sums[phase, chunk] = [last + step * j for j in range(depth + 1)]
        ready[chunk] = sums[phase, chunk][-1] + 1

    for chunk in range(CHUNKS):
        add_sum(-1, chunk, add_load(0, chunk, 0))
    for phase in range(PHASES):
        count = counts[level_of(phase)]
        for chunk in range(CHUNKS):
            start = max(busy, ready[chunk])
            busy = start + count
            items.append((start, count, phase, chunk))
            last = start + count - 1 + E_LAG
            if phase < ROOT:
                last = max(last, add_load(phase + 1, chunk, last))
            add_sum(phase, chunk, last)
    end = max(max(ticks[-1] for ticks in sums.values()), load_busy + LOAD_LAG * z_count) + 1
    return loads, items, sums, end


def solve_kernel(
    bits, heights, tile, z_count, row_live_ref, inner_live_ref, load_ref, factor_ref, link_ref,
    out_ref, wide, core_land, in_land, mid_land, mine, theirs, sums_sent, held, make_w, make_g, use_w, use_g,
    acc, right, front_land, front_src, given, term, cross, make_sem, use_sem, core_s, core_r, in_s, in_r, mid_s, mid_r,
    out_s, out_r, swap_s, swap_r, front_s, front_r, term_sem, term_s, up_r, down_r, given_r, end_s, end_r,
    cross_s, cross_r,
):
    loads, items, sums, end = plan(bits, heights, tile, z_count)
    counts = [height // tile for height in heights]
    most = max(counts)
    starts = [sum(counts[:level]) for level in range(LEVELS)]
    odd = max(counts[level_of(phase)] for phase in range(1, PHASES, 2))
    half = mine.shape[1]
    elem_at, front_at = lax.axis_index("elem"), lax.axis_index("front")
    z_at, core_at = elem_at // 2, elem_at % 2
    middle = z_count // 2
    low = (z_at < middle).astype(jnp.int32)
    depth = low * z_at + (1 - low) * (z_count - 1 - z_at)
    toward = 2 * low - 1
    is_outer, is_inner = depth == 0, depth == middle - 1
    sibling = {"elem": z_at * 2 + 1 - core_at}
    nearer = {"elem": (z_at + toward) * 2 + core_at}
    farther_at = (z_at - toward) * (depth > 0).astype(jnp.int32) + z_at * (depth == 0).astype(jnp.int32)
    farther = {"elem": farther_at * 2 + core_at}

    def partner(bit):
        low_part = front_at % (1 << bit)
        bit_now = front_at // (1 << bit) % 2
        high_part = front_at // (2 << bit) * (2 << bit)
        return {"front": high_part + (1 - bit_now) * (1 << bit) + low_part}

    elem_count = 2 * z_count
    inner = given.shape[2]
    per = inner // tile
    grain = half // z_count
    shares = [1 << bits[level] for level in range(LEVELS)]
    spread = [counts[level] % shares[level] == 0 for level in range(LEVELS)]
    own_tile = elem_at * per

    def takes(level, row_tile):
        mine_now = row_tile % counts[level] % shares[level] if spread[level] else row_tile // counts[level]
        return mine_now == front_at % shares[level]

    given[...] = jnp.zeros_like(given)
    all_bits = max(bits)
    barrier = pltpu.get_barrier_semaphore()

    def greet(device):
        pl.semaphore_signal(barrier, inc=1, device_id=device, device_id_type=MESH)

    most_share = 1 << all_bits
    for shift in range(1, elem_count * most_share):
        other = (elem_at * most_share + front_at % most_share + shift) % (elem_count * most_share)
        greet({"elem": other // most_share, "front": front_at - front_at % most_share + other % most_share})
    pl.semaphore_wait(barrier, elem_count * most_share - 1)

    def decode(tick):
        facts = [jnp.int32(0)] * 5
        for start, count, phase, chunk in items:
            hit = jnp.logical_and(tick >= start, tick < start + count)
            for at, value in enumerate((1, phase, chunk, start, starts[level_of(phase)])):
                if value:
                    facts[at] = jnp.where(hit, value, facts[at])
        return tuple(facts)

    def open_up(code, tick):
        valid, phase, chunk, start, first = code
        sub = tick - start
        return phase, chunk, sub, first + sub

    def is_valid(code):
        return code[0] == 1

    def mid_slot(phase, chunk, sub):
        return chunk * (most + odd) + phase % 2 * most + sub

    def remote(source, target, send, receive, device):
        return pltpu.make_async_remote_copy(
            src_ref=source, dst_ref=target, send_sem=send, recv_sem=receive, device_id=device, device_id_type=MESH
        )

    def core_copy(tick, slot):
        return remote(theirs.at[tick % (A_LAG + 1)], core_land.at[slot], core_s.at[slot], core_r.at[slot], sibling)

    def in_copy(tick, slot):
        return remote(sums_sent.at[tick % SENT], in_land.at[slot], in_s.at[slot], in_r.at[slot], nearer)

    def mid_copy(tick, slot):
        return remote(sums_sent.at[tick % SENT], mid_land.at[slot], mid_s.at[slot], mid_r.at[slot], nearer)

    def out_copy(slot):
        place = wide.at[slot, pl.ds(0, half)]
        return remote(place, place, out_s.at[slot], out_r.at[slot], farther)

    def swap_copy(slot):
        return remote(
            wide.at[slot, pl.ds(0, half)], wide.at[slot, pl.ds(half, half)], swap_s.at[slot], swap_r.at[slot], sibling
        )

    def factor_copy(buffer, sem, ring, block):
        at = pl.multiple_of(block * tile, tile)
        return pltpu.make_async_copy(factor_ref.at[pl.ds(at, tile), :], buffer.at[ring], sem.at[ring])

    def link_copy(buffer, sem, ring, block):
        at = pl.multiple_of(block * tile, tile)
        return pltpu.make_async_copy(link_ref.at[:, pl.ds(at, tile)], buffer.at[ring], sem.at[ring])

    def make_load(code, tick, act):
        phase, chunk, sub, block = open_up(code, tick)
        ring = tick % RING
        pl.when(phase <= ROOT)(lambda: act(factor_copy(make_w, make_sem, ring, block)))
        pl.when(phase > ROOT)(lambda: act(link_copy(make_g, make_sem, ring, block)))

    def use_load(code, tick, act):
        phase, chunk, sub, block = open_up(code, tick)
        ring = tick % RING
        pl.when(phase >= ROOT)(lambda: act(factor_copy(use_w, use_sem, ring, block)))
        pl.when(phase < ROOT)(lambda: act(link_copy(use_g, use_sem, ring, block)))

    def contract(left, right_value, axis):
        return lax.dot_general(left, right_value, (((1,), (axis,)), ((), ())), preferred_element_type=F32)

    span = LOAD_LAG * z_count
    rest = sum(counts[1:])

    def decode_load(tick):
        facts = [jnp.int32(0)] * 4
        for start, pairs, level, chunk in loads:
            hit = jnp.logical_and(tick >= start, tick < start + pairs)
            for at, value in enumerate((1, level, chunk, start)):
                if value:
                    facts[at] = jnp.where(hit, value, facts[at])
        return tuple(facts)

    def pick(level, values):
        result = values[0]
        for at in range(1, LEVELS):
            result = jnp.where(level == at, values[at], result)
        return result

    def row_tile_of(level, nth):
        place = front_at % shares[level]
        if not spread[level]:
            return place * counts[level] + nth
        each = counts[level] // shares[level]
        return nth // each * counts[level] + nth % each * shares[level] + place

    def open_load(code, tick):
        valid, level, chunk, start = code
        at = tick - start
        count = pick(level, counts)
        block = pick(level, starts)
        base = pick(level, [0] + [CHUNKS * most + starts[at] - counts[0] for at in range(1, LEVELS)])
        slot = base + chunk * jnp.where(level == 0, most, rest)
        kept = level * CHUNKS + chunk
        tiles = []
        for which in range(2):
            tile_at = at if which == 0 else count - 1 - at
            there = True if which == 0 else tile_at > at
            row_tile = pick(level, [row_tile_of(at_level, tile_at) for at_level in range(LEVELS)])
            owner = row_tile // per
            sub = row_tile % per
            ring = tick % span * 2 + which
            tiles.append((there, chunk, block + tile_at, slot + tile_at, kept, owner // 2, owner % 2, sub, ring))
        return tiles

    cross_base = {}
    for level in range(LEVELS):
        if spread[level] and shares[level] > 1:
            cross_base[level] = CHUNKS * sum(counts[other] for other in cross_base)

    def term_wait(ring):
        pltpu.make_async_copy(load_ref.at[0, :, pl.ds(0, tile)], term.at[ring], term_sem.at[ring]).wait()

    def cross_send(level, chunk, to, r, act):
        each = counts[level] // shares[level]
        place = front_at % shares[level]
        at = pl.multiple_of((starts[level] + r * shares[level] + to) * tile, tile)
        spot = cross_base[level] + chunk * counts[level] + place * each + r
        act(
            remote(
                load_ref.at[chunk, :, pl.ds(at, tile)], cross.at[spot],
                cross_s.at[cross_base[level] + chunk * counts[level] + r * shares[level] + to], cross_r.at[spot],
                {"front": front_at - place + to},
            )
        )

    def cross_sends(act):
        for level in cross_base:
            for chunk in range(CHUNKS):
                for r in range(counts[level] // shares[level]):
                    for to in range(shares[level]):
                        away = front_at % shares[level] != to
                        pl.when(away)(lambda level=level, chunk=chunk, to=to, r=r: cross_send(level, chunk, to, r, act))

    def term_start(level, chunk, nth, ring):
        for level_at in range(LEVELS):

            @pl.when(level == level_at)
            def _(level_at=level_at):
                count, place = counts[level_at], front_at % shares[level_at]
                crosses = level_at in cross_base
                row_tile = row_tile_of(level_at, nth)

                def from_here():
                    at = pl.multiple_of((starts[level_at] + row_tile % count) * tile, tile)
                    pltpu.make_async_copy(load_ref.at[chunk, :, pl.ds(at, tile)], term.at[ring], term_sem.at[ring]).start()

                if not crosses:
                    from_here()
                else:
                    pl.when(row_tile // count == place)(from_here)

                    @pl.when(row_tile // count != place)
                    def _():
                        spot = cross_base[level_at] + chunk * count + nth
                        remote(
                            load_ref.at[chunk, :, pl.ds(0, tile)], cross.at[spot], cross_s.at[spot], cross_r.at[spot], sibling
                        ).wait_recv()
                        pltpu.make_async_copy(cross.at[spot], term.at[ring], term_sem.at[ring]).start()

    upper = {"elem": (z_at + 1) % z_count * 2 + core_at}
    lower = {"elem": (z_at + z_count - 1) % z_count * 2 + core_at}

    def up_copy(ring, slot):
        return remote(term.at[ring], wide.at[slot, pl.ds(0, half)], term_s.at[ring], up_r.at[slot], upper)

    def down_copy(ring, slot):
        return remote(term.at[ring], wide.at[slot, pl.ds(half, half)], term_s.at[ring], down_r.at[slot], lower)

    def given_copy(ring, kept, sub):
        at = pl.multiple_of(sub * tile, tile)
        return remote(
            term.at[ring], given.at[kept, pl.ds(half, half), pl.ds(at, tile)], term_s.at[ring],
            given_r.at[kept * per + sub], sibling,
        )

    def load_retire(code, tick):
        for there, chunk, block, slot, kept, z_own, core_own, sub, ring in open_load(code, tick):
            leaves = jnp.logical_or(z_own != z_at, core_own != core_at)
            leaves = jnp.logical_and(there, leaves)
            pl.when(leaves)(lambda ring=ring, slot=slot: up_copy(ring, slot).wait_send())

    def load_start(code, tick):
        for there, chunk, block, slot, kept, z_own, core_own, sub, ring in open_load(code, tick):
            nth = block - pick(code[1], starts)
            go = functools.partial(term_start, code[1], chunk, nth, ring)
            go() if there is True else pl.when(there)(go)

    def add_land(ring, slot, side):
        total = term[ring].astype(F32) + wide[slot, pl.ds(side * half, half)].astype(F32)
        term[ring] = total.astype(BF)

    def load_stage(code, tick, stage):
        for there, chunk, block, slot, kept, z_own, core_own, sub, ring in open_load(code, tick):
            if stage < z_count - 1:
                rises = jnp.logical_and(there, jnp.logical_and(z_at < z_own, z_at == stage))
                falls = jnp.logical_and(there, jnp.logical_and(z_at > z_own, z_count - 1 - z_at == stage))

                @pl.when(rises)
                def _(chunk=chunk, block=block, slot=slot, ring=ring):
                    term_wait(ring)
                    if stage:
                        up_copy(ring, slot).wait_recv()
                        add_land(ring, slot, 0)
                    up_copy(ring, slot).start()

                @pl.when(falls)
                def _(chunk=chunk, block=block, slot=slot, ring=ring):
                    term_wait(ring)
                    if stage:
                        down_copy(ring, slot).wait_recv()
                        add_land(ring, slot, 1)
                    down_copy(ring, slot).start()

            else:

                @pl.when(jnp.logical_and(there, z_at == z_own))
                def _(chunk=chunk, block=block, slot=slot, kept=kept, core_own=core_own, sub=sub, ring=ring):
                    term_wait(ring)

                    @pl.when(z_at > 0)
                    def _():
                        up_copy(ring, slot).wait_recv()
                        add_land(ring, slot, 0)

                    @pl.when(z_at < z_count - 1)
                    def _():
                        down_copy(ring, slot).wait_recv()
                        add_land(ring, slot, 1)

                    @pl.when(core_own == core_at)
                    def _():
                        at = pl.multiple_of(sub * tile, tile)
                        given[kept, pl.ds(0, half), pl.ds(at, tile)] = term[ring]

                    @pl.when(core_own != core_at)
                    def _():
                        given_copy(ring, kept, sub).start()

    offsets = [starts[level] * tile for level in range(LEVELS)]

    parts = [min(share, inner // BLK) for share in shares]
    depths = [inner // part for part in parts]
    homes = [front_at - front_at % share + own_tile // counts[level] for level, share in enumerate(shares)]
    end_base = [CHUNKS * elem_count * sum(parts[:level]) for level in range(LEVELS)]
    sends = [front_at % share < part for share, part in zip(shares, parts)]

    def end_copy(level, chunk, side, z_to, sender, part):
        kept = level * CHUNKS + chunk
        depth_now = depths[level]
        at = offsets[level] + sender % (elem_count // shares[level]) * inner + part * depth_now
        at = pl.multiple_of(at, depth_now)
        core_to = core_at if side == 0 else 1 - core_at
        return remote(
            given.at[kept, pl.ds(side * half + z_to * grain, grain), pl.ds(pl.multiple_of(part * depth_now, depth_now), depth_now)],
            out_ref.at[pl.ds(pl.multiple_of(chunk * grain, grain), grain), pl.ds(at, depth_now)],
            end_s.at[kept * elem_count + z_to * 2 + side],
            end_r.at[end_base[level] + (chunk * elem_count + sender) * parts[level] + part],
            {"elem": z_to * 2 + core_to, "front": homes[level]},
        )

    def end_sends(level, chunk, act):
        for z_to in range(z_count):
            for side in range(2):
                copy = end_copy(level, chunk, side, z_to, elem_at, front_at % shares[level])
                if side:
                    act(copy)
                else:
                    away = jnp.logical_or(z_at != z_to, front_at != homes[level])
                    pl.when(away)(lambda copy=copy: act(copy))

    def end_keep(level, chunk):
        kept = level * CHUNKS + chunk
        depth_now = depths[level]
        part = front_at % shares[level] * depth_now
        at = pl.multiple_of(offsets[level] + elem_at % (elem_count // shares[level]) * inner + part, depth_now)
        rows = pl.ds(pl.multiple_of(chunk * grain, grain), grain)
        own = pl.ds(pl.multiple_of(z_at * grain, grain), grain)

        @pl.when(jnp.logical_and(front_at == homes[level], sends[level]))
        def _():
            out_ref[rows, pl.ds(at, depth_now)] = given[kept, own, pl.ds(pl.multiple_of(part, depth_now), depth_now)]

    def end_waits():
        for level in range(LEVELS):
            for chunk in range(CHUNKS):
                pl.when(sends[level])(lambda: end_sends(level, chunk, lambda copy: copy.wait_send()))
                senders = elem_count // shares[level]
                for nth in range(senders):
                    sender = front_at % shares[level] * senders + nth
                    for part in range(parts[level]):
                        own = jnp.logical_and(elem_at == sender, front_at % shares[level] == part)

                        @pl.when(jnp.logical_not(own))
                        def _():
                            end_copy(level, chunk, 1, 0, sender, part).wait_recv()

    def step_d(code, tick):
        phase, chunk, sub, block = open_up(code, tick)
        slot = chunk * most + sub

        @pl.when(jnp.logical_not(is_inner))
        def _():
            out_copy(slot).wait_recv()
            swap_copy(slot).start()
            pl.when(depth > 0)(lambda: out_copy(slot).start())

    def step_c(code, tick):
        phase, chunk, sub, block = open_up(code, tick)
        slot = chunk * most + sub
        mid = mid_slot(phase, chunk, sub)
        kept = chunk * starts[ROOT] + block

        @pl.when(is_inner)
        def _():
            mid_copy(tick, mid).wait()
            total = sums_sent[tick % SENT].astype(F32) + mid_land[mid].astype(F32)
            live = row_live_ref[block]

            @pl.when(phase <= ROOT)
            def _():
                value = (live * total).astype(BF)
                wide[slot, pl.ds(0, half)] = value

                @pl.when(phase < ROOT)
                def _():
                    held[kept] = value

            @pl.when(phase > ROOT)
            def _():
                wide[slot, pl.ds(0, half)] = (live * (held[kept].astype(F32) - total)).astype(BF)

            swap_copy(slot).start()
            if middle > 1:
                out_copy(slot).start()

        if middle > 2:

            @pl.when(jnp.logical_and(depth > 0, jnp.logical_not(is_inner)))
            def _():
                in_copy(tick, slot).wait_send()

    def step_b(code, tick):
        phase, chunk, sub, block = open_up(code, tick)
        slot = chunk * most + sub

        if middle > 1:

            @pl.when(is_outer)
            def _():
                in_copy(tick, slot).wait_send()

            @pl.when(depth > 0)
            def _():
                in_copy(tick, slot).wait_recv()
                sums_sent[tick % SENT] = (mine[tick % HELD] + in_land[slot].astype(F32)).astype(BF)
                pl.when(is_inner)(lambda: mid_copy(tick, mid_slot(phase, chunk, sub)).start())
                if middle > 2:
                    pl.when(jnp.logical_not(is_inner))(lambda: in_copy(tick, slot).start())

    def step_a(code, tick):
        phase, chunk, sub, block = open_up(code, tick)
        slot = chunk * most + sub

        core_copy(tick, slot).wait()

        @pl.when(is_outer)
        def _():
            sums_sent[tick % SENT] = (mine[tick % HELD] + core_land[slot].astype(F32)).astype(BF)
            if middle > 1:
                in_copy(tick, slot).start()
            else:
                mid_copy(tick, mid_slot(phase, chunk, sub)).start()

        @pl.when(depth > 0)
        def _():
            mine[tick % HELD] = mine[tick % HELD] + core_land[slot].astype(F32)

    def step_e(code, tick):
        phase, chunk, sub, block = open_up(code, tick)
        slot = chunk * most + sub
        ring = tick % RING
        use_load(code, tick, lambda copy: copy.wait())
        swap_copy(slot).wait()
        pl.when(depth > 0)(lambda: out_copy(slot).wait_send())

        @pl.when(sub == 0)
        def _():
            acc[chunk] = jnp.zeros(acc.shape[1:], F32)

        @pl.when(phase < ROOT)
        def _():
            acc[chunk] += contract(wide[slot], use_g[ring], 1)

        @pl.when(phase >= ROOT)
        def _():
            acc[chunk] += contract(wide[slot], use_w[ring], 0)

    lands, land_at = {}, 0
    for level in range(LEVELS):
        for j in range(bits[level]):
            lands[level, j] = land_at
            land_at += 1

    def front_copies(phase, j, target, chunk):
        count = bits[target]
        for part in range(2):
            bit = j if part == 0 else count - 1 - j
            rows = pl.ds(part * half, half)
            at = lands[target, j] * CHUNKS + chunk
            yield remote(
                front_src.at[chunk, rows], front_land.at[at, rows], front_s.at[at * 2 + part],
                front_r.at[at * 2 + part], partner(bit),
            )

    def finish(tick):
        for phase in range(-1, PHASES):
            target = target_of(phase)
            ticks = [sums[phase, chunk] for chunk in range(CHUNKS)]
            for j in range(bits[target] + 1):
                hits = [tick == ticks[chunk][j] for chunk in range(CHUNKS)]

                @pl.when(jnp.logical_or(*hits))
                def _(phase=phase, j=j, target=target, hits=hits):
                    chunk = hits[1].astype(jnp.int32)
                    kept = target * CHUNKS + chunk
                    if j == 0 and phase < ROOT:

                        for sub in range(per):

                            @pl.when(takes(target, own_tile + sub))
                            def _(sub=sub):
                                given_copy(0, kept, sub).wait_recv()

                        value = given[kept].astype(F32)
                        if phase >= 0:
                            value = value - acc[chunk]
                    else:
                        value = acc[chunk]
                    if j:
                        for copy in front_copies(phase, j - 1, target, chunk):
                            copy.wait()
                        value = value + front_land[lands[target, j - 1] * CHUNKS + chunk].astype(F32)
                    if j < bits[target]:
                        acc[chunk] = value
                        front_src[chunk] = value.astype(BF)
                        for copy in front_copies(phase, j, target, chunk):
                            copy.start()
                    else:
                        result = (inner_live_ref[target : target + 1, :] * value).astype(BF)
                        right[chunk] = result
                        if phase >= ROOT:
                            given[kept] = result

    def step_make(code, tick):
        phase, chunk, sub, block = open_up(code, tick)
        slot = chunk * most + sub
        ring = tick % RING
        make_load(code, tick, lambda copy: copy.wait())

        def place(product):
            mine[tick % HELD] = product[:half]
            theirs[tick % (A_LAG + 1)] = product[half:].astype(BF)

        @pl.when(phase <= ROOT)
        def _():
            place(contract(right[chunk], make_w[ring], 1))

        @pl.when(phase > ROOT)
        def _():
            place(contract(right[chunk], make_g[ring], 0))

        core_copy(tick, slot).start()

    made = max(start + count for start, count, phase, chunk in items) + SEND_GAP
    leaving = {}
    for level in range(LEVELS):
        for chunk in range(CHUNKS):
            leaving.setdefault(max(made, sums[2 * ROOT - level, chunk][-1]), []).append((level, chunk))

    def leave(tick):
        for at, group in leaving.items():
            for level, chunk in group:

                @pl.when(jnp.logical_and(tick == at, sends[level]))
                def _(level=level, chunk=chunk):
                    end_sends(level, chunk, lambda copy: copy.start())
                    end_keep(level, chunk)

    sum_ticks = sorted({at for ticks in sums.values() for at in ticks})

    def tick_body(tick, carry):
        codes, load_codes = carry
        codes = (decode(tick + 1),) + codes[:-1]
        load_codes = (decode_load(tick),) + load_codes[:-1]

        def guarded(code, step, *rest):
            pl.when(is_valid(code))(lambda: step(code, *rest))

        def start(copy):
            copy.start()

        guarded(codes[0], make_load, tick + 1, start)
        guarded(codes[E_LAG], use_load, tick + 1 - E_LAG, start)
        guarded(load_codes[span], load_retire, tick - span)
        guarded(load_codes[0], load_start, tick)
        for stage in range(z_count):
            lag = 1 + LOAD_LAG * stage
            guarded(load_codes[lag], load_stage, tick - lag, stage)
        guarded(codes[D_LAG + 1], step_d, tick - D_LAG)
        guarded(codes[C_LAG + 1], step_c, tick - C_LAG)
        guarded(codes[B_LAG + 1], step_b, tick - B_LAG)
        guarded(codes[A_LAG + 1], step_a, tick - A_LAG)
        guarded(codes[E_LAG + 1], step_e, tick - E_LAG)
        hit = tick == sum_ticks[0]
        for at in sum_ticks[1:]:
            hit = jnp.logical_or(hit, tick == at)
        pl.when(hit)(lambda: finish(tick))
        guarded(codes[1], step_make, tick)
        pl.when(tick >= made)(lambda: leave(tick))
        return codes, load_codes

    nothing = tuple([tuple([jnp.int32(0)] * 5)] * (E_LAG + 2))
    no_load = tuple([tuple([jnp.int32(0)] * 4)] * (span + 1))
    cross_sends(lambda copy: copy.start())
    lax.fori_loop(0, end, tick_body, (nothing, no_load))
    cross_sends(lambda copy: copy.wait_send())
    end_waits()


def solve(loads, row_live, inner_live, factor, links, bits, heights, z_count):
    half, inner = loads.shape[1], links.shape[0]
    wide_columns = 2 * half
    tile = min(TILE, min(heights))
    counts = [height // tile for height in heights]
    most = max(counts)
    odd = max(counts[level_of(phase)] for phase in range(1, PHASES, 2))
    slots = CHUNKS * most
    load_slots = CHUNKS * sum(counts)
    mids = CHUNKS * (most + odd)
    lands = CHUNKS * sum(bits)
    kept = CHUNKS * sum(counts[:ROOT])
    crossed = max(1, CHUNKS * sum(count for count, bit in zip(counts, bits) if bit and count % (1 << bit) == 0))
    ends = LEVELS * CHUNKS * 2 * z_count
    lives = row_live.reshape(sum(counts), 1, tile)
    dma = pltpu.SemaphoreType.DMA
    vmem = pltpu.VMEM
    in_vmem, anywhere = pl.BlockSpec(memory_space=pltpu.VMEM), pl.BlockSpec(memory_space=pl.ANY)
    kernel = functools.partial(solve_kernel, bits, heights, tile, z_count)
    flops = 4 * wide_columns * CHUNKS * (factor.size + links.size)
    return pl.pallas_call(
        kernel,
        out_shape=jax.ShapeDtypeStruct((CHUNKS * half // z_count, factor.shape[0]), BF),
        in_specs=[in_vmem] * 2 + [anywhere] * 3,
        out_specs=in_vmem,
        scratch_shapes=[
            vmem((load_slots, wide_columns, tile), BF),
            vmem((slots, half, tile), BF),
            vmem((slots, half, tile), BF),
            vmem((mids, half, tile), BF),
            vmem((HELD, half, tile), F32),
            vmem((A_LAG + 1, half, tile), BF),
            vmem((SENT, half, tile), BF),
            vmem((kept, half, tile), BF),
            vmem((RING, tile, inner), BF),
            vmem((RING, inner, tile), BF),
            vmem((RING, tile, inner), BF),
            vmem((RING, inner, tile), BF),
            vmem((CHUNKS, wide_columns, inner), F32),
            vmem((CHUNKS, wide_columns, inner), BF),
            vmem((lands, wide_columns, inner), BF),
            vmem((CHUNKS, wide_columns, inner), BF),
            vmem((LEVELS * CHUNKS, wide_columns, inner), BF),
            vmem((2 * LOAD_LAG * z_count, half, tile), BF),
            vmem((crossed, half, tile), BF),
            dma((RING,)),
            dma((RING,)),
            dma((slots,)),
            dma((slots,)),
            dma((slots,)),
            dma((slots,)),
            dma((mids,)),
            dma((mids,)),
            dma((slots,)),
            dma((slots,)),
            dma((slots,)),
            dma((slots,)),
            dma((2 * lands,)),
            dma((2 * lands,)),
            dma((2 * LOAD_LAG * z_count,)),
            dma((2 * LOAD_LAG * z_count,)),
            dma((load_slots,)),
            dma((load_slots,)),
            dma((LEVELS * CHUNKS * (inner // tile),)),
            dma((ends,)),
            dma((CHUNKS * 2 * z_count * sum(1 << bit for bit in bits),)),
            dma((crossed,)),
            dma((crossed,)),
        ],
        cost_estimate=pl.CostEstimate(flops=flops, bytes_accessed=8 * (factor.size + links.size), transcendentals=0),
        compiler_params=pltpu.CompilerParams(
            collective_id=0, has_side_effects=True, vmem_limit_bytes=63 * 1024 * 1024
        ),
    )(lives, inner_live, loads, factor, links)


def body(
    elem_mat, elem_deriv, elem_disp, elem_sens, design_var, dof_rows, inverse_factor, coupling, front_sizes
):
    depth_bits = lax.axis_size("front").bit_length() - 1
    elem_count = lax.axis_size("elem")
    z_count = elem_count // 2
    device = lax.axis_index("front")
    elem_at = lax.axis_index("elem")
    z_at, core_at = elem_at // 2, elem_at % 2
    inner = coupling.shape[0]
    solve_size = inner * elem_count
    spot_rows = inverse_factor.shape[0]
    columns = elem_sens.shape[2]
    own_columns = columns // elem_count
    grain = own_columns // CHUNKS
    half = z_count * grain

    def core_swap(value):
        return lax.ppermute(value, "elem", [(i, i ^ 1) for i in range(elem_count)])

    facts = []
    offset = 0
    first_front = 0
    for level_at in range(LEVELS):
        bit_count = depth_bits - (LEVELS - 1 - level_at)
        block_rows = solve_size >> bit_count
        front_id = first_front + (device >> bit_count)
        size_now = lax.dynamic_index_in_dim(front_sizes, front_id, 0, keepdims=False)
        start = (device & (1 << bit_count) - 1) * block_rows
        row_live = (start + lax.iota(jnp.int32, block_rows) < size_now).astype(F32)[None, :]
        inner_live = (elem_at * inner + lax.iota(jnp.int32, inner) < size_now).astype(F32)[None, :]
        facts.append((bit_count, block_rows, offset, row_live, inner_live))
        offset = offset + block_rows
        first_front = first_front + (1 << LEVELS - 1 - level_at)

    place = lax.iota(jnp.int32, columns)
    place_core, rest = place // (z_count * own_columns), place % (z_count * own_columns)
    place_chunk, rest = rest // half, rest % half
    column_ids = (rest // grain * 2 + place_core) * own_columns + place_chunk * grain + rest % grain
    order = (place[:, None] == column_ids[None, :]).astype(BF)
    sens = jnp.einsum("ejc,cd->ejd", elem_sens, order, preferred_element_type=F32).astype(BF)

    pseudo = local_pseudo(elem_mat, elem_deriv, elem_disp, sens, design_var, column_ids).astype(BF)
    side = columns // 2
    own_pseudo = lax.dynamic_slice_in_dim(pseudo, core_at * side, side, 2)
    other_pseudo = core_swap(lax.dynamic_slice_in_dim(pseudo, (1 - core_at) * side, side, 2))
    places = jnp.concatenate([dof_rows, core_swap(dof_rows)], 1)
    blocks, rows = block_places(places, spot_rows)

    loads = scatter_rows(own_pseudo, other_pseudo, blocks, rows, spot_rows)
    row_live = jnp.concatenate([fact[3] for fact in facts], 1)
    inner_live = jnp.concatenate([fact[4] for fact in facts], 0)
    bits, heights = [fact[0] for fact in facts], [fact[1] for fact in facts]
    answers = solve(loads, row_live, inner_live, inverse_factor, coupling, bits, heights, z_count)
    return answers.astype(F32).T


def solution(mesh):
    return jax.shard_map(
        body,
        mesh=mesh,
        in_specs=(
            P(None, None, ("elem", "front")),
            P(None, None, ("elem", "front")),
            P(None, ("elem", "front")),
            P(("elem", "front"), None, None),
            P(("elem", "front")),
            P(None, ("elem", "front")),
            P("front", "elem"),
            P("elem", "front"),
            P(),
        ),
        out_specs=P("front", "elem"),
        check_vma=False,
    )
```

```python
import functools

import jax
import jax.numpy as jnp
from jax import lax
from jax.experimental import pallas as pl
from jax.experimental.pallas import tpu as pltpu
from jax.sharding import PartitionSpec as P

LEVELS = 3
CHUNKS = 2
TILE = 512
RING = 2
HELD = 4
SENT = 8
TURN = 512
SEND_GAP = 3
LOAD_LAG = 2
BLK = 128
GROUP = 8
BF, F32 = jnp.bfloat16, jnp.float32


def local_pseudo(tables, derivs, disps, sens, variables, column_ids):
    pseudo = -jnp.einsum("ije,ejc->eic", tables, sens, preferred_element_type=F32)
    drive_term = -jnp.einsum("ije,je->ei", derivs, disps, preferred_element_type=F32)
    hit_column = (column_ids[None, :] == variables[:, None]).astype(F32)
    return pseudo + drive_term[:, :, None] * hit_column[:, None, :]


def scatter_kernel(blocks_ref, rows_ref, own_ref, other_ref, out_ref, total):
    total[...] = jnp.zeros_like(total)
    count, dof = own_ref.shape[0], rows_ref.shape[1]

    for source_at, source_ref in enumerate((own_ref, other_ref)):

        def step(group_at, carry):
            first = pl.multiple_of(group_at * GROUP, GROUP)
            entry = pl.multiple_of(source_at * count + first, GROUP)
            rows = rows_ref[pl.ds(entry, GROUP), :]
            spread = []
            for at in range(GROUP):
                lanes = jnp.broadcast_to(rows[at : at + 1, :], (BLK, dof))
                hits = lax.broadcasted_iota(jnp.int32, (BLK, dof), 0) == lanes
                spread.append(
                    jnp.dot(hits.astype(F32).astype(BF), source_ref[first + at], preferred_element_type=F32)
                )
            for at in range(GROUP):
                block = blocks_ref[entry + at]
                total[block] = total[block] + spread[at]
            return carry

        lax.fori_loop(0, count // GROUP, step, 0)

    lanes = total.shape[2]
    same = lax.broadcasted_iota(jnp.int32, (lanes, lanes), 0) == lax.broadcasted_iota(jnp.int32, (lanes, lanes), 1)
    unit = same.astype(F32).astype(BF)
    turned = TURN // BLK
    width = lanes // CHUNKS

    def turn(step, carry):
        at = pl.multiple_of(step * TURN, TURN)
        piece = total[pl.ds(step * turned, turned)].reshape(TURN, lanes).astype(BF)
        moved = lax.dot_general(unit, piece, (((1,), (1,)), ((), ())), preferred_element_type=F32).astype(BF)
        for chunk in range(CHUNKS):
            out_ref[chunk, :, pl.ds(at, TURN)] = moved[chunk * width : (chunk + 1) * width]
        return carry

    lax.fori_loop(0, total.shape[0] // turned, turn, 0)


def block_places(places, spot_rows):
    places = places.T
    used = places < spot_rows
    blocks = jnp.min(jnp.where(used, places, spot_rows), 1) // BLK
    blocks = jnp.clip(blocks, 0, spot_rows // BLK - 1)
    rows = jnp.where(used, places - blocks[:, None] * BLK, -1)
    return blocks, rows


def scatter_rows(own, other, blocks, rows, spot_rows):
    width = own.shape[2]
    vmem = pl.BlockSpec(memory_space=pltpu.VMEM)
    return pl.pallas_call(
        scatter_kernel,
        out_shape=jax.ShapeDtypeStruct((CHUNKS, width // CHUNKS, spot_rows), BF),
        in_specs=[pl.BlockSpec(memory_space=pltpu.SMEM), vmem, vmem, vmem],
        out_specs=vmem,
        scratch_shapes=[pltpu.VMEM((spot_rows // BLK, BLK, width), F32)],
        compiler_params=pltpu.CompilerParams(vmem_limit_bytes=40 * 1024 * 1024),
    )(blocks, rows, own, other)


A_LAG, B_LAG, C_LAG, D_LAG, E_LAG = 1, 3, 5, 7, 8
PHASES = 2 * LEVELS - 1
ROOT = LEVELS - 1
MESH = pl.DeviceIdType.MESH


def level_of(phase):
    return phase if phase <= ROOT else 2 * ROOT - phase


def target_of(phase):
    return phase + 1 if phase < ROOT else level_of(phase)


def plan(bits, heights, tile, z_count):
    counts = [height // tile for height in heights]
    loads, items, sums, busy, load_busy = [], [], {}, 0, 0
    ready = [0] * CHUNKS

    def add_load(level, chunk, wanted):
        nonlocal load_busy
        count = (counts[level] + 1) // 2
        start = max(load_busy, wanted - count - 1 - LOAD_LAG * (z_count - 1))
        load_busy = start + count
        loads.append((start, count, level, chunk))
        return load_busy - 1 + LOAD_LAG * (z_count - 1) + 2

    def add_sum(phase, chunk, last):
        depth = bits[target_of(phase)]
        step = 4 if depth == 1 else 3
        sums[phase, chunk] = [last + step * j for j in range(depth + 1)]
        ready[chunk] = sums[phase, chunk][-1] + 1

    for chunk in range(CHUNKS):
        add_sum(-1, chunk, add_load(0, chunk, 0))
    for phase in range(PHASES):
        count = counts[level_of(phase)]
        for chunk in range(CHUNKS):
            start = max(busy, ready[chunk])
            busy = start + count
            items.append((start, count, phase, chunk))
            last = start + count - 1 + E_LAG
            if phase < ROOT:
                last = max(last, add_load(phase + 1, chunk, last))
            add_sum(phase, chunk, last)
    end = max(max(ticks[-1] for ticks in sums.values()), load_busy + LOAD_LAG * z_count) + 1
    return loads, items, sums, end


def solve_kernel(
    bits, heights, tile, z_count, row_live_ref, inner_live_ref, load_ref, factor_ref, link_ref,
    out_ref, wide, core_land, in_land, mid_land, mine, theirs, sums_sent, held, make_w, make_g, use_w, use_g,
    acc, right, front_land, front_src, given, term, cross, make_sem, use_sem, core_s, core_r, in_s, in_r, mid_s, mid_r,
    out_s, out_r, swap_s, swap_r, front_s, front_r, term_sem, term_s, up_r, down_r, given_r, end_s, end_r,
    cross_s, cross_r,
):
    loads, items, sums, end = plan(bits, heights, tile, z_count)
    counts = [height // tile for height in heights]
    most = max(counts)
    starts = [sum(counts[:level]) for level in range(LEVELS)]
    odd = max(counts[level_of(phase)] for phase in range(1, PHASES, 2))
    half = mine.shape[1]
    elem_at, front_at = lax.axis_index("elem"), lax.axis_index("front")
    z_at, core_at = elem_at // 2, elem_at % 2
    middle = z_count // 2
    low = (z_at < middle).astype(jnp.int32)
    depth = low * z_at + (1 - low) * (z_count - 1 - z_at)
    toward = 2 * low - 1
    is_outer, is_inner = depth == 0, depth == middle - 1
    sibling = {"elem": z_at * 2 + 1 - core_at}
    nearer = {"elem": (z_at + toward) * 2 + core_at}
    farther_at = (z_at - toward) * (depth > 0).astype(jnp.int32) + z_at * (depth == 0).astype(jnp.int32)
    farther = {"elem": farther_at * 2 + core_at}

    def partner(bit):
        low_part = front_at % (1 << bit)
        bit_now = front_at // (1 << bit) % 2
        high_part = front_at // (2 << bit) * (2 << bit)
        return {"front": high_part + (1 - bit_now) * (1 << bit) + low_part}

    elem_count = 2 * z_count
    inner = given.shape[2]
    per = inner // tile
    grain = half // z_count
    shares = [1 << bits[level] for level in range(LEVELS)]
    spread = [counts[level] % shares[level] == 0 for level in range(LEVELS)]
    own_tile = elem_at * per

    def takes(level, row_tile):
        mine_now = row_tile % counts[level] % shares[level] if spread[level] else row_tile // counts[level]
        return mine_now == front_at % shares[level]

    given[...] = jnp.zeros_like(given)
    all_bits = max(bits)
    barrier = pltpu.get_barrier_semaphore()

    def greet(device):
        pl.semaphore_signal(barrier, inc=1, device_id=device, device_id_type=MESH)

    most_share = 1 << all_bits
    for shift in range(1, elem_count * most_share):
        other = (elem_at * most_share + front_at % most_share + shift) % (elem_count * most_share)
        greet({"elem": other // most_share, "front": front_at - front_at % most_share + other % most_share})
    pl.semaphore_wait(barrier, elem_count * most_share - 1)

    def decode(tick):
        facts = [jnp.int32(0)] * 5
        for start, count, phase, chunk in items:
            hit = jnp.logical_and(tick >= start, tick < start + count)
            for at, value in enumerate((1, phase, chunk, start, starts[level_of(phase)])):
                if value:
                    facts[at] = jnp.where(hit, value, facts[at])
        return tuple(facts)

    def open_up(code, tick):
        valid, phase, chunk, start, first = code
        sub = tick - start
        return phase, chunk, sub, first + sub

    def is_valid(code):
        return code[0] == 1

    def mid_slot(phase, chunk, sub):
        return chunk * (most + odd) + phase % 2 * most + sub

    def remote(source, target, send, receive, device):
        return pltpu.make_async_remote_copy(
            src_ref=source, dst_ref=target, send_sem=send, recv_sem=receive, device_id=device, device_id_type=MESH
        )

    def core_copy(tick, slot):
        return remote(theirs.at[tick % (A_LAG + 1)], core_land.at[slot], core_s.at[slot], core_r.at[slot], sibling)

    def in_copy(tick, slot):
        return remote(sums_sent.at[tick % SENT], in_land.at[slot], in_s.at[slot], in_r.at[slot], nearer)

    def mid_copy(tick, slot):
        return remote(sums_sent.at[tick % SENT], mid_land.at[slot], mid_s.at[slot], mid_r.at[slot], nearer)

    def out_copy(slot):
        place = wide.at[slot, pl.ds(0, half)]
        return remote(place, place, out_s.at[slot], out_r.at[slot], farther)

    def swap_copy(slot):
        return remote(
            wide.at[slot, pl.ds(0, half)], wide.at[slot, pl.ds(half, half)], swap_s.at[slot], swap_r.at[slot], sibling
        )

    def factor_copy(buffer, sem, ring, block):
        at = pl.multiple_of(block * tile, tile)
        return pltpu.make_async_copy(factor_ref.at[pl.ds(at, tile), :], buffer.at[ring], sem.at[ring])

    def link_copy(buffer, sem, ring, block):
        at = pl.multiple_of(block * tile, tile)
        return pltpu.make_async_copy(link_ref.at[:, pl.ds(at, tile)], buffer.at[ring], sem.at[ring])

    def make_load(code, tick, act):
        phase, chunk, sub, block = open_up(code, tick)
        ring = tick % RING
        pl.when(phase <= ROOT)(lambda: act(factor_copy(make_w, make_sem, ring, block)))
        pl.when(phase > ROOT)(lambda: act(link_copy(make_g, make_sem, ring, block)))

    def use_load(code, tick, act):
        phase, chunk, sub, block = open_up(code, tick)
        ring = tick % RING
        pl.when(phase >= ROOT)(lambda: act(factor_copy(use_w, use_sem, ring, block)))
        pl.when(phase < ROOT)(lambda: act(link_copy(use_g, use_sem, ring, block)))

    def contract(left, right_value, axis):
        return lax.dot_general(left, right_value, (((1,), (axis,)), ((), ())), preferred_element_type=F32)

    span = LOAD_LAG * z_count
    rest = sum(counts[1:])

    def decode_load(tick):
        facts = [jnp.int32(0)] * 4
        for start, pairs, level, chunk in loads:
            hit = jnp.logical_and(tick >= start, tick < start + pairs)
            for at, value in enumerate((1, level, chunk, start)):
                if value:
                    facts[at] = jnp.where(hit, value, facts[at])
        return tuple(facts)

    def pick(level, values):
        result = values[0]
        for at in range(1, LEVELS):
            result = jnp.where(level == at, values[at], result)
        return result

    def row_tile_of(level, nth):
        place = front_at % shares[level]
        if not spread[level]:
            return place * counts[level] + nth
        each = counts[level] // shares[level]
        return nth // each * counts[level] + nth % each * shares[level] + place

    def open_load(code, tick):
        valid, level, chunk, start = code
        at = tick - start
        count = pick(level, counts)
        block = pick(level, starts)
        base = pick(level, [0] + [CHUNKS * most + starts[at] - counts[0] for at in range(1, LEVELS)])
        slot = base + chunk * jnp.where(level == 0, most, rest)
        kept = level * CHUNKS + chunk
        tiles = []
        for which in range(2):
            tile_at = at if which == 0 else count - 1 - at
            there = True if which == 0 else tile_at > at
            row_tile = pick(level, [row_tile_of(at_level, tile_at) for at_level in range(LEVELS)])
            owner = row_tile // per
            sub = row_tile % per
            ring = tick % span * 2 + which
            tiles.append((there, chunk, block + tile_at, slot + tile_at, kept, owner // 2, owner % 2, sub, ring))
        return tiles

    cross_base = {}
    for level in range(LEVELS):
        if spread[level] and shares[level] > 1:
            cross_base[level] = CHUNKS * sum(counts[other] for other in cross_base)

    def term_wait(ring):
        pltpu.make_async_copy(load_ref.at[0, :, pl.ds(0, tile)], term.at[ring], term_sem.at[ring]).wait()

    def cross_send(level, chunk, to, r, act):
        each = counts[level] // shares[level]
        place = front_at % shares[level]
        at = pl.multiple_of((starts[level] + r * shares[level] + to) * tile, tile)
        spot = cross_base[level] + chunk * counts[level] + place * each + r
        act(
            remote(
                load_ref.at[chunk, :, pl.ds(at, tile)], cross.at[spot],
                cross_s.at[cross_base[level] + chunk * counts[level] + r * shares[level] + to], cross_r.at[spot],
                {"front": front_at - place + to},
            )
        )

    def cross_sends(act):
        for level in cross_base:
            for chunk in range(CHUNKS):
                for r in range(counts[level] // shares[level]):
                    for to in range(shares[level]):
                        away = front_at % shares[level] != to
                        pl.when(away)(lambda level=level, chunk=chunk, to=to, r=r: cross_send(level, chunk, to, r, act))

    def term_start(level, chunk, nth, ring):
        for level_at in range(LEVELS):

            @pl.when(level == level_at)
            def _(level_at=level_at):
                count, place = counts[level_at], front_at % shares[level_at]
                crosses = level_at in cross_base
                row_tile = row_tile_of(level_at, nth)

                def from_here():
                    at = pl.multiple_of((starts[level_at] + row_tile % count) * tile, tile)
                    pltpu.make_async_copy(load_ref.at[chunk, :, pl.ds(at, tile)], term.at[ring], term_sem.at[ring]).start()

                if not crosses:
                    from_here()
                else:
                    pl.when(row_tile // count == place)(from_here)

                    @pl.when(row_tile // count != place)
                    def _():
                        spot = cross_base[level_at] + chunk * count + nth
                        remote(
                            load_ref.at[chunk, :, pl.ds(0, tile)], cross.at[spot], cross_s.at[spot], cross_r.at[spot], sibling
                        ).wait_recv()
                        pltpu.make_async_copy(cross.at[spot], term.at[ring], term_sem.at[ring]).start()

    upper = {"elem": (z_at + 1) % z_count * 2 + core_at}
    lower = {"elem": (z_at + z_count - 1) % z_count * 2 + core_at}

    def up_copy(ring, slot):
        return remote(term.at[ring], wide.at[slot, pl.ds(0, half)], term_s.at[ring], up_r.at[slot], upper)

    def down_copy(ring, slot):
        return remote(term.at[ring], wide.at[slot, pl.ds(half, half)], term_s.at[ring], down_r.at[slot], lower)

    def given_copy(ring, kept, sub):
        at = pl.multiple_of(sub * tile, tile)
        return remote(
            term.at[ring], given.at[kept, pl.ds(half, half), pl.ds(at, tile)], term_s.at[ring],
            given_r.at[kept * per + sub], sibling,
        )

    def load_retire(code, tick):
        for there, chunk, block, slot, kept, z_own, core_own, sub, ring in open_load(code, tick):
            leaves = jnp.logical_or(z_own != z_at, core_own != core_at)
            leaves = jnp.logical_and(there, leaves)
            pl.when(leaves)(lambda ring=ring, slot=slot: up_copy(ring, slot).wait_send())

    def load_start(code, tick):
        for there, chunk, block, slot, kept, z_own, core_own, sub, ring in open_load(code, tick):
            nth = block - pick(code[1], starts)
            go = functools.partial(term_start, code[1], chunk, nth, ring)
            go() if there is True else pl.when(there)(go)

    def add_land(ring, slot, side):
        total = term[ring].astype(F32) + wide[slot, pl.ds(side * half, half)].astype(F32)
        term[ring] = total.astype(BF)

    def load_stage(code, tick, stage):
        for there, chunk, block, slot, kept, z_own, core_own, sub, ring in open_load(code, tick):
            if stage < z_count - 1:
                rises = jnp.logical_and(there, jnp.logical_and(z_at < z_own, z_at == stage))
                falls = jnp.logical_and(there, jnp.logical_and(z_at > z_own, z_count - 1 - z_at == stage))

                @pl.when(rises)
                def _(chunk=chunk, block=block, slot=slot, ring=ring):
                    term_wait(ring)
                    if stage:
                        up_copy(ring, slot).wait_recv()
                        add_land(ring, slot, 0)
                    up_copy(ring, slot).start()

                @pl.when(falls)
                def _(chunk=chunk, block=block, slot=slot, ring=ring):
                    term_wait(ring)
                    if stage:
                        down_copy(ring, slot).wait_recv()
                        add_land(ring, slot, 1)
                    down_copy(ring, slot).start()

            else:

                @pl.when(jnp.logical_and(there, z_at == z_own))
                def _(chunk=chunk, block=block, slot=slot, kept=kept, core_own=core_own, sub=sub, ring=ring):
                    term_wait(ring)

                    @pl.when(z_at > 0)
                    def _():
                        up_copy(ring, slot).wait_recv()
                        add_land(ring, slot, 0)

                    @pl.when(z_at < z_count - 1)
                    def _():
                        down_copy(ring, slot).wait_recv()
                        add_land(ring, slot, 1)

                    @pl.when(core_own == core_at)
                    def _():
                        at = pl.multiple_of(sub * tile, tile)
                        given[kept, pl.ds(0, half), pl.ds(at, tile)] = term[ring]

                    @pl.when(core_own != core_at)
                    def _():
                        given_copy(ring, kept, sub).start()

    offsets = [starts[level] * tile for level in range(LEVELS)]

    parts = [min(share, inner // BLK) for share in shares]
    depths = [inner // part for part in parts]
    homes = [front_at - front_at % share + own_tile // counts[level] for level, share in enumerate(shares)]
    end_base = [CHUNKS * elem_count * sum(parts[:level]) for level in range(LEVELS)]
    sends = [front_at % share < part for share, part in zip(shares, parts)]

    def end_copy(level, chunk, side, z_to, sender, part):
        kept = level * CHUNKS + chunk
        depth_now = depths[level]
        at = offsets[level] + sender % (elem_count // shares[level]) * inner + part * depth_now
        at = pl.multiple_of(at, depth_now)
        core_to = core_at if side == 0 else 1 - core_at
        return remote(
            given.at[kept, pl.ds(side * half + z_to * grain, grain), pl.ds(pl.multiple_of(part * depth_now, depth_now), depth_now)],
            out_ref.at[pl.ds(pl.multiple_of(chunk * grain, grain), grain), pl.ds(at, depth_now)],
            end_s.at[kept * elem_count + z_to * 2 + side],
            end_r.at[end_base[level] + (chunk * elem_count + sender) * parts[level] + part],
            {"elem": z_to * 2 + core_to, "front": homes[level]},
        )

    def end_sends(level, chunk, act):
        for z_to in range(z_count):
            for side in range(2):
                copy = end_copy(level, chunk, side, z_to, elem_at, front_at % shares[level])
                if side:
                    act(copy)
                else:
                    away = jnp.logical_or(z_at != z_to, front_at != homes[level])
                    pl.when(away)(lambda copy=copy: act(copy))

    def end_keep(level, chunk):
        kept = level * CHUNKS + chunk
        depth_now = depths[level]
        part = front_at % shares[level] * depth_now
        at = pl.multiple_of(offsets[level] + elem_at % (elem_count // shares[level]) * inner + part, depth_now)
        rows = pl.ds(pl.multiple_of(chunk * grain, grain), grain)
        own = pl.ds(pl.multiple_of(z_at * grain, grain), grain)

        @pl.when(jnp.logical_and(front_at == homes[level], sends[level]))
        def _():
            out_ref[rows, pl.ds(at, depth_now)] = given[kept, own, pl.ds(pl.multiple_of(part, depth_now), depth_now)]

    def end_waits():
        for level in range(LEVELS):
            for chunk in range(CHUNKS):
                pl.when(sends[level])(lambda: end_sends(level, chunk, lambda copy: copy.wait_send()))
                senders = elem_count // shares[level]
                for nth in range(senders):
                    sender = front_at % shares[level] * senders + nth
                    for part in range(parts[level]):
                        own = jnp.logical_and(elem_at == sender, front_at % shares[level] == part)

                        @pl.when(jnp.logical_not(own))
                        def _():
                            end_copy(level, chunk, 1, 0, sender, part).wait_recv()

    def step_d(code, tick):
        phase, chunk, sub, block = open_up(code, tick)
        slot = chunk * most + sub

        @pl.when(jnp.logical_not(is_inner))
        def _():
            out_copy(slot).wait_recv()
            swap_copy(slot).start()
            pl.when(depth > 0)(lambda: out_copy(slot).start())

    def step_c(code, tick):
        phase, chunk, sub, block = open_up(code, tick)
        slot = chunk * most + sub
        mid = mid_slot(phase, chunk, sub)
        kept = chunk * starts[ROOT] + block

        @pl.when(is_inner)
        def _():
            mid_copy(tick, mid).wait()
            total = sums_sent[tick % SENT].astype(F32) + mid_land[mid].astype(F32)
            live = row_live_ref[block]

            @pl.when(phase <= ROOT)
            def _():
                value = (live * total).astype(BF)
                wide[slot, pl.ds(0, half)] = value

                @pl.when(phase < ROOT)
                def _():
                    held[kept] = value

            @pl.when(phase > ROOT)
            def _():
                wide[slot, pl.ds(0, half)] = (live * (held[kept].astype(F32) - total)).astype(BF)

            swap_copy(slot).start()
            if middle > 1:
                out_copy(slot).start()

        if middle > 2:

            @pl.when(jnp.logical_and(depth > 0, jnp.logical_not(is_inner)))
            def _():
                in_copy(tick, slot).wait_send()

    def step_b(code, tick):
        phase, chunk, sub, block = open_up(code, tick)
        slot = chunk * most + sub

        if middle > 1:

            @pl.when(is_outer)
            def _():
                in_copy(tick, slot).wait_send()

            @pl.when(depth > 0)
            def _():
                in_copy(tick, slot).wait_recv()
                sums_sent[tick % SENT] = (mine[tick % HELD] + in_land[slot].astype(F32)).astype(BF)
                pl.when(is_inner)(lambda: mid_copy(tick, mid_slot(phase, chunk, sub)).start())
                if middle > 2:
                    pl.when(jnp.logical_not(is_inner))(lambda: in_copy(tick, slot).start())

    def step_a(code, tick):
        phase, chunk, sub, block = open_up(code, tick)
        slot = chunk * most + sub

        core_copy(tick, slot).wait()

        @pl.when(is_outer)
        def _():
            sums_sent[tick % SENT] = (mine[tick % HELD] + core_land[slot].astype(F32)).astype(BF)
            if middle > 1:
                in_copy(tick, slot).start()
            else:
                mid_copy(tick, mid_slot(phase, chunk, sub)).start()

        @pl.when(depth > 0)
        def _():
            mine[tick % HELD] = mine[tick % HELD] + core_land[slot].astype(F32)

    def step_e(code, tick):
        phase, chunk, sub, block = open_up(code, tick)
        slot = chunk * most + sub
        ring = tick % RING
        use_load(code, tick, lambda copy: copy.wait())
        swap_copy(slot).wait()
        pl.when(depth > 0)(lambda: out_copy(slot).wait_send())

        @pl.when(sub == 0)
        def _():
            acc[chunk] = jnp.zeros(acc.shape[1:], F32)

        @pl.when(phase < ROOT)
        def _():
            acc[chunk] += contract(wide[slot], use_g[ring], 1)

        @pl.when(phase >= ROOT)
        def _():
            acc[chunk] += contract(wide[slot], use_w[ring], 0)

    lands, land_at = {}, 0
    for level in range(LEVELS):
        for j in range(bits[level]):
            lands[level, j] = land_at
            land_at += 1

    def front_copies(phase, j, target, chunk):
        count = bits[target]
        for part in range(2):
            bit = j if part == 0 else count - 1 - j
            rows = pl.ds(part * half, half)
            at = lands[target, j] * CHUNKS + chunk
            yield remote(
                front_src.at[chunk, rows], front_land.at[at, rows], front_s.at[at * 2 + part],
                front_r.at[at * 2 + part], partner(bit),
            )

    def finish(tick):
        for phase in range(-1, PHASES):
            target = target_of(phase)
            ticks = [sums[phase, chunk] for chunk in range(CHUNKS)]
            for j in range(bits[target] + 1):
                hits = [tick == ticks[chunk][j] for chunk in range(CHUNKS)]

                @pl.when(jnp.logical_or(*hits))
                def _(phase=phase, j=j, target=target, hits=hits):
                    chunk = hits[1].astype(jnp.int32)
                    kept = target * CHUNKS + chunk
                    if j == 0 and phase < ROOT:

                        for sub in range(per):

                            @pl.when(takes(target, own_tile + sub))
                            def _(sub=sub):
                                given_copy(0, kept, sub).wait_recv()

                        value = given[kept].astype(F32)
                        if phase >= 0:
                            value = value - acc[chunk]
                    else:
                        value = acc[chunk]
                    if j:
                        for copy in front_copies(phase, j - 1, target, chunk):
                            copy.wait()
                        value = value + front_land[lands[target, j - 1] * CHUNKS + chunk].astype(F32)
                    if j < bits[target]:
                        acc[chunk] = value
                        front_src[chunk] = value.astype(BF)
                        for copy in front_copies(phase, j, target, chunk):
                            copy.start()
                    else:
                        result = (inner_live_ref[target : target + 1, :] * value).astype(BF)
                        right[chunk] = result
                        if phase >= ROOT:
                            given[kept] = result

    def step_make(code, tick):
        phase, chunk, sub, block = open_up(code, tick)
        slot = chunk * most + sub
        ring = tick % RING
        make_load(code, tick, lambda copy: copy.wait())

        def place(product):
            mine[tick % HELD] = product[:half]
            theirs[tick % (A_LAG + 1)] = product[half:].astype(BF)

        @pl.when(phase <= ROOT)
        def _():
            place(contract(right[chunk], make_w[ring], 1))

        @pl.when(phase > ROOT)
        def _():
            place(contract(right[chunk], make_g[ring], 0))

        core_copy(tick, slot).start()

    made = max(start + count for start, count, phase, chunk in items) + SEND_GAP
    leaving = {}
    for level in range(LEVELS):
        for chunk in range(CHUNKS):
            leaving.setdefault(max(made, sums[2 * ROOT - level, chunk][-1]), []).append((level, chunk))

    def leave(tick):
        for at, group in leaving.items():
            for level, chunk in group:

                @pl.when(jnp.logical_and(tick == at, sends[level]))
                def _(level=level, chunk=chunk):
                    end_sends(level, chunk, lambda copy: copy.start())
                    end_keep(level, chunk)

    sum_ticks = sorted({at for ticks in sums.values() for at in ticks})

    def tick_body(tick, carry):
        codes, load_codes = carry
        codes = (decode(tick + 1),) + codes[:-1]
        load_codes = (decode_load(tick),) + load_codes[:-1]

        def guarded(code, step, *rest):
            pl.when(is_valid(code))(lambda: step(code, *rest))

        def start(copy):
            copy.start()

        guarded(codes[0], make_load, tick + 1, start)
        guarded(codes[E_LAG], use_load, tick + 1 - E_LAG, start)
        guarded(load_codes[span], load_retire, tick - span)
        guarded(load_codes[0], load_start, tick)
        guarded(codes[D_LAG + 1], step_d, tick - D_LAG)
        guarded(codes[C_LAG + 1], step_c, tick - C_LAG)
        guarded(codes[B_LAG + 1], step_b, tick - B_LAG)
        guarded(codes[A_LAG + 1], step_a, tick - A_LAG)
        guarded(codes[E_LAG + 1], step_e, tick - E_LAG)
        hit = tick == sum_ticks[0]
        for at in sum_ticks[1:]:
            hit = jnp.logical_or(hit, tick == at)
        pl.when(hit)(lambda: finish(tick))
        guarded(codes[1], step_make, tick)
        for stage in range(z_count):
            lag = 1 + LOAD_LAG * stage
            guarded(load_codes[lag], load_stage, tick - lag, stage)
        pl.when(tick >= made)(lambda: leave(tick))
        return codes, load_codes

    nothing = tuple([tuple([jnp.int32(0)] * 5)] * (E_LAG + 2))
    no_load = tuple([tuple([jnp.int32(0)] * 4)] * (span + 1))
    cross_sends(lambda copy: copy.start())
    lax.fori_loop(0, end, tick_body, (nothing, no_load))
    cross_sends(lambda copy: copy.wait_send())
    end_waits()


def solve(loads, row_live, inner_live, factor, links, bits, heights, z_count):
    half, inner = loads.shape[1], links.shape[0]
    wide_columns = 2 * half
    tile = min(TILE, min(heights))
    counts = [height // tile for height in heights]
    most = max(counts)
    odd = max(counts[level_of(phase)] for phase in range(1, PHASES, 2))
    slots = CHUNKS * most
    load_slots = CHUNKS * sum(counts)
    mids = CHUNKS * (most + odd)
    lands = CHUNKS * sum(bits)
    kept = CHUNKS * sum(counts[:ROOT])
    crossed = max(1, CHUNKS * sum(count for count, bit in zip(counts, bits) if bit and count % (1 << bit) == 0))
    ends = LEVELS * CHUNKS * 2 * z_count
    lives = row_live.reshape(sum(counts), 1, tile)
    dma = pltpu.SemaphoreType.DMA
    vmem = pltpu.VMEM
    in_vmem, anywhere = pl.BlockSpec(memory_space=pltpu.VMEM), pl.BlockSpec(memory_space=pl.ANY)
    kernel = functools.partial(solve_kernel, bits, heights, tile, z_count)
    flops = 4 * wide_columns * CHUNKS * (factor.size + links.size)
    return pl.pallas_call(
        kernel,
        out_shape=jax.ShapeDtypeStruct((CHUNKS * half // z_count, factor.shape[0]), BF),
        in_specs=[in_vmem] * 2 + [anywhere] * 3,
        out_specs=in_vmem,
        scratch_shapes=[
            vmem((load_slots, wide_columns, tile), BF),
            vmem((slots, half, tile), BF),
            vmem((slots, half, tile), BF),
            vmem((mids, half, tile), BF),
            vmem((HELD, half, tile), F32),
            vmem((A_LAG + 1, half, tile), BF),
            vmem((SENT, half, tile), BF),
            vmem((kept, half, tile), BF),
            vmem((RING, tile, inner), BF),
            vmem((RING, inner, tile), BF),
            vmem((RING, tile, inner), BF),
            vmem((RING, inner, tile), BF),
            vmem((CHUNKS, wide_columns, inner), F32),
            vmem((CHUNKS, wide_columns, inner), BF),
            vmem((lands, wide_columns, inner), BF),
            vmem((CHUNKS, wide_columns, inner), BF),
            vmem((LEVELS * CHUNKS, wide_columns, inner), BF),
            vmem((2 * LOAD_LAG * z_count, half, tile), BF),
            vmem((crossed, half, tile), BF),
            dma((RING,)),
            dma((RING,)),
            dma((slots,)),
            dma((slots,)),
            dma((slots,)),
            dma((slots,)),
            dma((mids,)),
            dma((mids,)),
            dma((slots,)),
            dma((slots,)),
            dma((slots,)),
            dma((slots,)),
            dma((2 * lands,)),
            dma((2 * lands,)),
            dma((2 * LOAD_LAG * z_count,)),
            dma((2 * LOAD_LAG * z_count,)),
            dma((load_slots,)),
            dma((load_slots,)),
            dma((LEVELS * CHUNKS * (inner // tile),)),
            dma((ends,)),
            dma((CHUNKS * 2 * z_count * sum(1 << bit for bit in bits),)),
            dma((crossed,)),
            dma((crossed,)),
        ],
        cost_estimate=pl.CostEstimate(flops=flops, bytes_accessed=8 * (factor.size + links.size), transcendentals=0),
        compiler_params=pltpu.CompilerParams(
            collective_id=0, has_side_effects=True, vmem_limit_bytes=63 * 1024 * 1024
        ),
    )(lives, inner_live, loads, factor, links)


def body(
    elem_mat, elem_deriv, elem_disp, elem_sens, design_var, dof_rows, inverse_factor, coupling, front_sizes
):
    depth_bits = lax.axis_size("front").bit_length() - 1
    elem_count = lax.axis_size("elem")
    z_count = elem_count // 2
    device = lax.axis_index("front")
    elem_at = lax.axis_index("elem")
    z_at, core_at = elem_at // 2, elem_at % 2
    inner = coupling.shape[0]
    solve_size = inner * elem_count
    spot_rows = inverse_factor.shape[0]
    columns = elem_sens.shape[2]
    own_columns = columns // elem_count
    grain = own_columns // CHUNKS
    half = z_count * grain

    def core_swap(value):
        return lax.ppermute(value, "elem", [(i, i ^ 1) for i in range(elem_count)])

    facts = []
    offset = 0
    first_front = 0
    for level_at in range(LEVELS):
        bit_count = depth_bits - (LEVELS - 1 - level_at)
        block_rows = solve_size >> bit_count
        front_id = first_front + (device >> bit_count)
        size_now = lax.dynamic_index_in_dim(front_sizes, front_id, 0, keepdims=False)
        start = (device & (1 << bit_count) - 1) * block_rows
        row_live = (start + lax.iota(jnp.int32, block_rows) < size_now).astype(F32)[None, :]
        inner_live = (elem_at * inner + lax.iota(jnp.int32, inner) < size_now).astype(F32)[None, :]
        facts.append((bit_count, block_rows, offset, row_live, inner_live))
        offset = offset + block_rows
        first_front = first_front + (1 << LEVELS - 1 - level_at)

    place = lax.iota(jnp.int32, columns)
    place_core, rest = place // (z_count * own_columns), place % (z_count * own_columns)
    place_chunk, rest = rest // half, rest % half
    column_ids = (rest // grain * 2 + place_core) * own_columns + place_chunk * grain + rest % grain
    order = (place[:, None] == column_ids[None, :]).astype(BF)
    sens = jnp.einsum("ejc,cd->ejd", elem_sens, order, preferred_element_type=F32).astype(BF)

    pseudo = local_pseudo(elem_mat, elem_deriv, elem_disp, sens, design_var, column_ids).astype(BF)
    side = columns // 2
    own_pseudo = lax.dynamic_slice_in_dim(pseudo, core_at * side, side, 2)
    other_pseudo = core_swap(lax.dynamic_slice_in_dim(pseudo, (1 - core_at) * side, side, 2))
    places = jnp.concatenate([dof_rows, core_swap(dof_rows)], 1)
    blocks, rows = block_places(places, spot_rows)

    loads = scatter_rows(own_pseudo, other_pseudo, blocks, rows, spot_rows)
    row_live = jnp.concatenate([fact[3] for fact in facts], 1)
    inner_live = jnp.concatenate([fact[4] for fact in facts], 0)
    bits, heights = [fact[0] for fact in facts], [fact[1] for fact in facts]
    answers = solve(loads, row_live, inner_live, inverse_factor, coupling, bits, heights, z_count)
    return answers.astype(F32).T


def solution(mesh):
    return jax.shard_map(
        body,
        mesh=mesh,
        in_specs=(
            P(None, None, ("elem", "front")),
            P(None, None, ("elem", "front")),
            P(None, ("elem", "front")),
            P(("elem", "front"), None, None),
            P(("elem", "front")),
            P(None, ("elem", "front")),
            P("front", "elem"),
            P("elem", "front"),
            P(),
        ),
        out_specs=P("front", "elem"),
        check_vma=False,
    )
```
